32 devices in a mesh: groups: 2 (over y), date: 4 (over z), row: 2 (over core), col: 2 (over x).
Axes of the slice: x: 2, y: 2, z: 4, core: 2. Of those that a mesh axis runs over, the one named last changes fastest.
Arguments:
- pixels: bfloat16 [8, 2, 13, 384, 192], P(('groups', 'date'), None, None, 'row', 'col'), parts along dimension 0, may hold values from -6 to 6
- w_stem: bfloat16 [64, 13, 7, 7], replicated, may hold values from -0.25 to 0.25
- w_head: float32 [64, 128], replicated, may hold values from -0.75 to 0.75
- pool_grid: int32 [192, 96], P('row', 'col'), may hold values from 0 to 71, as said below
- neg_index: int32 [8, 2, 24, 12, 128], P(('groups', 'date'), None, 'row', 'col'), parts along dimension 0, may hold values from 0 to 143
- key_date: int32 [4], replicated, may hold values from 0 to 3, as said below
Outputs:
- anchor_loss: float32 [8, 2, 24, 12], P(('groups', 'date'), None, 'row', 'col'), parts along dimension 0
- grad_stem: float32 [128, 13, 7, 7], P('groups'), parts along dimension 0
- grad_head: float32 [128, 128], P('groups'), parts along dimension 0
The draws below stay inside these ranges and needn't reach their ends.
There are 2 independent parts, one for each index of `groups`. The reference program is written for one: setup_inputs(seed, part) draws one part's arguments, and reference() takes and returns one part's arrays. A program takes and returns all parts, laid end to end along the dimension named above; an argument that names none is the same for every part. Nothing has to cross between parts.
Inputs may be any that keep to these rules, and one draw needn't show every extreme that they name: `pool_grid`: cell numbers are local to a device block of 96 x 48 stem outputs; every block names each of its 72 cells at least once. `neg_index`: entry k names key k = t * 72 + c of the same block: cell c of tile t on the paired date. Following d to key_date[d] runs once through all 4 dates and back; no date is its own key date.
All inputs are finite; a program needn't handle non-finite values.
Results may differ from the reference program's by a relative error of at most 0.0052.
Values may be sent and summed in bfloat16 or wider, within the bound.
A program may use at most 128 MiB of HBM per device.

```python
import math
import jax
import jax.numpy as jnp
from jax import lax

BANDS = 13
CH = 64
EMB = 128
TILES = 2
CELL = 8
NEG = 128
DATES = 4
FH = 96
FW = 48
CELLS_DEV = 72
KEYS = 144
CELLS_R = 24
CELLS_C = 12
FEAT_H = 192
FEAT_W = 96
TILE_H = 384
TILE_W = 192
N_ROW = 2
N_COL = 2


def draw_pool_grid(key, part):
    row_ids = jnp.arange(FEAT_H, dtype=jnp.int32)[:, None] % FH
    col_ids = jnp.arange(FEAT_W, dtype=jnp.int32)[None, :] % FW
    regular = row_ids // CELL * (FW // CELL) + col_ids // CELL
    corner = jnp.logical_and(row_ids % CELL == 0, col_ids % CELL == 0)
    first_key, second_key = jax.random.split(jax.random.fold_in(key, 17))
    moving = jax.random.randint(first_key, (FEAT_H, FEAT_W), 0, 4) == 0
    other = jax.random.randint(second_key, (FEAT_H, FEAT_W), 0, CELLS_DEV)
    chosen = jnp.where(jnp.logical_and(moving, jnp.logical_not(corner)), other, regular)
    return chosen.astype(jnp.int32)


def draw_key_date(key, part):
    first_key, second_key = jax.random.split(jax.random.fold_in(key, 29))
    values = jnp.arange(DATES, dtype=jnp.int32)
    fixed = jnp.array([0, DATES - 1, DATES // 2 - 1, DATES // 2], dtype=jnp.int32)
    order = jax.random.permutation(first_key, values)
    place = jnp.zeros((DATES,), jnp.int32).at[order].set(values)
    fixed_hit = values[:, None] == fixed[None, :]
    fixed_rank = jnp.sum(jnp.where(fixed_hit, jnp.arange(4, dtype=jnp.int32)[None, :], 0), axis=1)
    score = jnp.where(jnp.any(fixed_hit, axis=1), fixed_rank, 4 + place)
    sequence = jnp.argsort(score, stable=True).astype(jnp.int32)
    start = jax.random.randint(second_key, (), 0, DATES)
    sequence = (sequence + start) % DATES
    following = jnp.roll(sequence, -1)
    return jnp.zeros((DATES,), jnp.int32).at[sequence].set(following)


def with_ends(values, own_key, low, top_value):
    longest = values.shape.index(max(values.shape))
    spots = []
    for shift in (0, 1):
        where = [jax.random.randint(jax.random.fold_in(own_key, axis), (), 0, length) for axis, length in enumerate(values.shape)]
        where[longest] = (where[longest] + shift) % values.shape[longest]
        spots.append(tuple(where))
    return values.at[spots[0]].set(low).at[spots[1]].set(top_value)


def shard_levels(own_key, extent, shards, low, largest):
    def one(axis_at, shards_of):
        heights = jax.random.uniform(jax.random.fold_in(jax.random.fold_in(own_key, 6), axis_at), (shards_of,), jnp.float32, low / len(shards), largest / len(shards))
        return jnp.repeat(jnp.exp(heights), extent[axis_at] // shards_of).reshape((-1,) + (1,) * (len(extent) - axis_at - 1))

    loudness = one(*shards[0])
    for cut in shards[1:]:
        loudness = loudness * one(*cut)
    return loudness


def gaussian(own_key, shape, deviation, limit, cuts=(), kind=jnp.bfloat16):
    entries = jax.random.normal(own_key, shape, jnp.float32) * deviation
    if len(cuts) > 0:
        entries = shard_levels(own_key, shape, cuts, -0.22, 0.18) * entries
    return jnp.clip(entries, min=-limit, max=limit).astype(kind)


def setup_inputs(seed: int = 0, part: int = 0) -> dict:
    arg_keys = jax.random.split(jax.random.key(seed), 7)
    own_keys = jax.random.split(jax.random.fold_in(arg_keys[6], part), 7)
    return {
        "pixels": gaussian(own_keys[0], (DATES, TILES, BANDS, TILE_H, TILE_W), 1.0, 6.0, ((0, 4), (3, 2), (4, 2))),
        "w_stem": gaussian(arg_keys[1], (CH, BANDS, 7, 7), (BANDS * 49) ** -0.5, 0.25),
        "w_head": gaussian(arg_keys[2], (CH, EMB), CH ** -0.5, 0.75, (), jnp.float32),
        "pool_grid": draw_pool_grid(jax.random.fold_in(arg_keys[6], 71), part),
        "neg_index": with_ends(jax.random.randint(own_keys[4], (DATES, TILES, CELLS_R, CELLS_C, NEG), 0, KEYS), jax.random.fold_in(own_keys[4], 1), 0, KEYS - 1).astype(jnp.int32),
        "key_date": draw_key_date(jax.random.fold_in(arg_keys[6], 71), part),
    }


TEMP = 0.2
EPS = 1e-06

def stem_conv(padded, w_stem):
    return lax.conv_general_dilated(padded, w_stem, (2, 2), 'VALID', dimension_numbers=('NCHW', 'OIHW', 'NCHW'), preferred_element_type=jnp.float32)

def weight_term(padded, slope_low):
    left_side = jnp.transpose(padded, (1, 0, 2, 3))
    right_side = jnp.transpose(slope_low, (1, 0, 2, 3))
    result = lax.conv_general_dilated(left_side, right_side, (1, 1), 'VALID', rhs_dilation=(2, 2), dimension_numbers=('NCHW', 'OIHW', 'NCHW'), preferred_element_type=jnp.float32)
    return jnp.transpose(result, (1, 0, 2, 3))

def to_blocks(feature):
    shaped = feature.reshape(TILES, CH, N_ROW, FH, N_COL, FW)
    return shaped.transpose(2, 4, 0, 1, 3, 5).reshape(N_ROW, N_COL, TILES, CH, FH * FW)

def from_blocks(blocked):
    shaped = blocked.reshape(N_ROW, N_COL, TILES, CH, FH, FW)
    return shaped.transpose(2, 3, 0, 4, 1, 5).reshape(TILES, CH, FEAT_H, FEAT_W)

def reference(pixels, w_stem, w_head, pool_grid, neg_index, key_date):
    anchors = KEYS
    grid_blocks = pool_grid.reshape(N_ROW, FH, N_COL, FW).transpose(0, 2, 1, 3).reshape(N_ROW, N_COL, FH * FW)
    member = (grid_blocks[..., None] == jnp.arange(CELLS_DEV, dtype=jnp.int32)).astype(jnp.float32)
    counts = lax.optimization_barrier(jnp.sum(member, axis=2))

    def pad_tile(tile_data):
        return jnp.pad(tile_data, ((0, 0), (0, 0), (3, 2), (3, 2)))

    def forward_date(tile_data):
        stem_out = stem_conv(pad_tile(tile_data), w_stem)
        hidden = lax.optimization_barrier(jnp.maximum(stem_out, 0.0).astype(jnp.bfloat16)).astype(jnp.float32)
        cell_sums = jnp.einsum('rstcp,rspk->rstkc', to_blocks(hidden), member, precision=lax.Precision.HIGHEST)
        return cell_sums / counts[:, :, None, :, None]
    pooled = lax.map(forward_date, pixels).reshape(DATES, N_ROW, N_COL, anchors, CH)
    project = jnp.einsum('drsac,ce->drsae', pooled, w_head, precision=lax.Precision.HIGHEST)
    length = jnp.sqrt(lax.optimization_barrier(jnp.sum(project * project, axis=-1, keepdims=True)) + EPS)
    embed = project / length
    date_ids = jnp.arange(DATES, dtype=jnp.int32)
    source_date = jnp.zeros((DATES,), jnp.int32).at[key_date].set(date_ids)
    key_rows = embed[key_date]
    scores = jnp.einsum('drsae,drsbe->drsab', embed, key_rows, precision=lax.Precision.HIGHEST) / TEMP
    neg_rows = neg_index.reshape(DATES, TILES, N_ROW, FH // CELL, N_COL, FW // CELL, NEG)
    neg_rows = neg_rows.transpose(0, 2, 4, 1, 3, 5, 6).reshape(DATES, N_ROW, N_COL, anchors, NEG)
    negative = jnp.take_along_axis(scores, neg_rows, axis=-1)
    positive = jnp.diagonal(scores, axis1=-2, axis2=-1)
    denominator = jnp.exp(positive) + lax.optimization_barrier(jnp.sum(jnp.exp(negative), axis=-1))
    losses = jnp.log(denominator) - positive
    anchor_loss = losses.reshape(DATES, N_ROW, N_COL, TILES, FH // CELL, FW // CELL)
    anchor_loss = anchor_loss.transpose(0, 3, 1, 4, 2, 5).reshape(DATES, TILES, CELLS_R, CELLS_C)
    scale = 1.0 / math.sqrt(DATES * TILES * CELLS_R * CELLS_C)
    d_pos = scale * (jnp.exp(positive) / denominator - 1.0)
    d_neg = scale * jnp.exp(negative) / denominator[..., None]
    arange_rows = jnp.arange(anchors, dtype=jnp.int32)

    def scatter_one(rows_one, neg_one, pos_one):
        grid_zero = jnp.zeros((anchors, anchors), jnp.float32)
        grid_zero = grid_zero.at[arange_rows[:, None], rows_one].add(neg_one)
        return grid_zero.at[arange_rows, arange_rows].add(pos_one)
    d_scores = jax.vmap(scatter_one)(neg_rows.reshape(-1, anchors, NEG), d_neg.reshape(-1, anchors, NEG), d_pos.reshape(-1, anchors))
    d_scores = d_scores.reshape(DATES, N_ROW, N_COL, anchors, anchors) / TEMP
    grad_anchor = jnp.einsum('drsab,drsbe->drsae', d_scores, key_rows, precision=lax.Precision.HIGHEST)
    grad_keys = jnp.einsum('drsab,drsae->drsbe', d_scores, embed, precision=lax.Precision.HIGHEST)
    grad_embed = grad_anchor + grad_keys[source_date]
    grad_project = (grad_embed - embed * lax.optimization_barrier(jnp.sum(embed * grad_embed, axis=-1, keepdims=True))) / length
    grad_head = jnp.einsum('drsac,drsae->ce', pooled, grad_project, precision=lax.Precision.HIGHEST)
    grad_pooled = jnp.einsum('drsae,ce->drsac', grad_project, w_head, precision=lax.Precision.HIGHEST)
    per_cell = grad_pooled.reshape(DATES, N_ROW, N_COL, TILES, CELLS_DEV, CH) / counts[None, :, :, None, :, None]

    def backward_date(carry, inputs):
        tile_data, cell_grad = inputs
        padded = pad_tile(tile_data)
        stem_out = stem_conv(padded, w_stem)
        spread = jnp.einsum('rstkc,rspk->rstcp', cell_grad, member, precision=lax.Precision.HIGHEST)
        slope_low = jnp.where(stem_out > 0, from_blocks(spread), 0.0).astype(jnp.bfloat16)
        return (carry + weight_term(padded, slope_low), None)
    grad_stem, _ = lax.scan(backward_date, jnp.zeros((CH, BANDS, 7, 7), jnp.float32), (pixels, per_cell))
    return (anchor_loss, grad_stem, grad_head)
```

```python
import functools
import math

import jax
import jax.numpy as jnp
import numpy as np
from jax import lax
from jax.experimental import pallas as pl
from jax.experimental.pallas import tpu as pltpu
from jax.sharding import PartitionSpec as P

CELL = 8
TEMP = 0.2
EPS = 1e-06
STEP = 24
LANES = 128
HALF = 64

MESH = pl.DeviceIdType.MESH
HIGH = lax.Precision.HIGHEST
BF = jnp.bfloat16
F32 = jnp.float32
KEY = F32


def mm(left, right):
    return lax.dot_general(left, right, (((1,), (0,)), ((), ())), preferred_element_type=F32)


def mm_high(left, right):
    return lax.dot_general(
        left, right, (((1,), (0,)), ((), ())), precision=HIGH, preferred_element_type=F32
    )


def fold(array):
    half = array.shape[0] // 2
    return jnp.concatenate([array[:half], array[half:]], axis=1)


def unfold(array):
    half = array.shape[1] // 2
    return jnp.concatenate([array[:, :half], array[:, half:]], axis=0)


def mm_nt(left, right, precision=None):
    return lax.dot_general(
        left, right, (((1,), (1,)), ((), ())), precision=precision, preferred_element_type=F32
    )


def mm_tn(left, right, precision=None):
    return lax.dot_general(
        left, right, (((0,), (0,)), ((), ())), precision=precision, preferred_element_type=F32
    )


def tables(tiles, bands, height, width):
    cols = np.zeros((tiles, width, 2 * LANES), np.float32)
    for t in range(tiles):
        for w in range(width):
            q = w + 3
            cols[t, w, (q % 2) * LANES + t * HALF + q // 2] = 1
    edge = np.zeros((tiles, 32, width), np.float32)
    halo = np.zeros((2, 16, 2 * LANES), np.float32)
    for t in range(tiles):
        for k in range(3):
            edge[t, t * 8 + k, width - 3 + k] = 1
            edge[t, 16 + t * 8 + k, k] = 1
            halo[0, t * 8 + k, (k % 2) * LANES + t * HALF + k // 2] = 1
            q = width + 3 + k
            halo[1, t * 8 + k, (q % 2) * LANES + t * HALF + q // 2] = 1
    rows = np.zeros((16, 16, 2, bands, 16), np.float32)
    for r in range(16):
        for c in range(bands):
            if r < 3:
                rows[r, c, 0, c, 13 + r] = 1
            else:
                rows[r, c, 1, c, r - 3] = 1
    rows = rows.reshape(256, 2 * bands * 16)
    taps = np.zeros((4, bands, 7, 8, 8, 2, 16), np.float32)
    for b in range(4):
        for c in range(bands):
            for u in range(7):
                for pc in range(2):
                    if 2 * b + pc < 7:
                        taps[b, c, u, 2 * b + pc, u, pc, c] = 1
    taps = taps.reshape(4, bands * 56, 256)
    return [jnp.asarray(x, BF) for x in (cols, edge, halo, rows, taps)]


def kernel(
    sizes,
    *refs,
):
    n_in = 12
    sources, outs = refs[:n_in], refs[n_in : n_in + 3]
    held, rest = refs[n_in + 3 : 2 * n_in + 3], refs[2 * n_in + 3 :]
    body(sizes, sources, held, *outs, *held, *rest)


def body(
    sizes, sources, held, loss_out, stem_out, head_out,
    pix, edge, w_taps, taps, grid_t, place, neg, cols, halo, rows, w_head, key_date,
    pack, strips, blocks, image, w_all, gids, neg_t, count_t, count_s, negs, member, hidden,
    keys, g_acc, part, got_1, got_2, got_3, got_4, h_own, h_part, h_got_1, h_got_2, h_got_3, h_got_4,
    s_col, r_col, s_row, r_row, s_key, r_key, s_neg, r_neg, s_1, r_1, s_2, r_2, s_3, r_3, s_4, r_4,
    s_h1, r_h1, s_h2, r_h2, s_h3, r_h3, s_h4, r_h4, s_in,
):
    tiles, bands, height, width, n_row, n_col, dates = sizes
    fr, fc = height // 2, width // 2
    cells = fr // CELL * (fc // CELL)
    anchors = tiles * cells
    n_mem = n_row * n_col
    row, col, date = lax.axis_index("row"), lax.axis_index("col"), lax.axis_index("date")

    fetches = [pltpu.make_async_copy(a, b, s_in.at[i]) for i, (a, b) in enumerate(zip(sources, held))]
    for c in fetches:
        c.start()
    barrier = pltpu.get_barrier_semaphore()

    def others(name, count, mine):
        found = []
        for k in range(1, count):
            other = lax.rem(mine + k, count)
            found.append((other, {name: other}))
        return found

    rows_of, cols_of = others("row", n_row, row), others("col", n_col, col)
    peers = others("date", dates, date)
    for _, dev in rows_of + cols_of + peers:
        pl.semaphore_signal(barrier, inc=1, device_id=dev, device_id_type=MESH)

    fetches[0].wait()
    fetches[1].wait()

    def pack_band(c, carry):
        both = mm_nt(edge[0], pix[0, c])
        for t in range(1, tiles):
            both += mm_nt(edge[t], pix[t, c])
        both = both.astype(BF)
        pack[0, c] = both[:16]
        pack[1, c] = both[16:]
        return carry

    lax.fori_loop(0, bands, pack_band, 0, unroll=True)
    pl.semaphore_wait(barrier, len(rows_of) + len(cols_of) + len(peers))

    def copy(src, dst, send, recv, dev):
        return pltpu.make_async_remote_copy(
            src_ref=src, dst_ref=dst, send_sem=send, recv_sem=recv,
            device_id=dev, device_id_type=MESH,
        )

    to_right = copy(pack.at[0], strips.at[0], s_col.at[0], r_col.at[0], {"col": lax.rem(col + 1, n_col)})
    to_left = copy(pack.at[1], strips.at[1], s_col.at[1], r_col.at[1], {"col": lax.rem(col + n_col - 1, n_col)})
    down = copy(blocks.at[height // 16], blocks.at[0], s_row.at[0], r_row.at[0], {"row": lax.rem(row + 1, n_row)})
    up = copy(blocks.at[1], blocks.at[height // 16 + 1], s_row.at[1], r_row.at[1], {"row": lax.rem(row + n_row - 1, n_row)})

    @pl.when(col < n_col - 1)
    def _():
        to_right.start()

    @pl.when(col > 0)
    def _():
        to_left.start()

    @pl.when(col == 0)
    def _():
        strips[0] = jnp.zeros(strips.shape[1:], BF)

    @pl.when(col == n_col - 1)
    def _():
        strips[1] = jnp.zeros(strips.shape[1:], BF)

    for c in fetches[2:]:
        c.wait()
    negs[pl.ds(date, 1)] = neg[...].astype(F32).astype(BF)[None]
    sends = [copy(negs.at[date], negs.at[date], s_neg.at[o], r_neg.at[date], dev) for o, dev in peers]
    for c in sends:
        c.start()
    w_flat = w_taps[...].astype(F32)
    w_flat = jnp.concatenate([w_flat, jnp.zeros((bands, 7, 1, 64), F32)], axis=2)
    w_flat = w_flat.reshape(bands * 56, 64).astype(BF)
    for b in range(4):
        w_all[64 * b : 64 * b + 64, :] = mm_tn(w_flat, taps[b]).astype(BF)
    lane = lax.broadcasted_iota(jnp.int32, (1, LANES), 1)
    inside = lax.rem(lane, HALF) < fc
    shift = jnp.where(inside, (lane // HALF) * cells, -1000).astype(F32)
    gids[...] = mm_tn(grid_t[...].astype(F32).astype(BF), place[...]) + shift
    sub = lax.broadcasted_iota(jnp.int32, (anchors, 1), 0)
    key_ids = (lax.rem(sub, tiles) * cells + sub // tiles).astype(F32)
    eye_n = (
        lax.broadcasted_iota(jnp.int32, (neg.shape[1],) * 2, 0)
        == lax.broadcasted_iota(jnp.int32, (neg.shape[1],) * 2, 1)
    ).astype(F32).astype(BF)

    def count_keys(index):
        neg_t[...] = mm_nt(eye_n, index)

        def count_step(s, total):
            for k in range(8):
                total += jnp.where(neg_t[pl.ds(s * 8 + k, 1), :] == key_ids, 1.0, 0.0)
            return total

        return lax.fori_loop(
            0, neg.shape[1] // 8, count_step, jnp.zeros((anchors, anchors), F32)
        )

    count_t[...] = count_keys(negs[date])

    @pl.when(col > 0)
    def _():
        copy(pack.at[0], strips.at[0], s_col.at[0], r_col.at[0], {"col": lax.rem(col + n_col - 1, n_col)}).wait_recv()

    @pl.when(col < n_col - 1)
    def _():
        copy(pack.at[1], strips.at[1], s_col.at[1], r_col.at[1], {"col": lax.rem(col + 1, n_col)}).wait_recv()

    def own_band(c, carry):
        wide = mm_tn(strips[0, c], halo[0]) + mm_tn(strips[1, c], halo[1])
        for t in range(tiles):
            wide += mm(pix[t, c], cols[t])
        blocks[pl.ds(1, height // 16), c] = wide.astype(BF).reshape(height // 16, 16, 2 * LANES)
        return carry

    lax.fori_loop(0, bands, own_band, 0, unroll=True)

    @pl.when(row < n_row - 1)
    def _():
        down.start()

    @pl.when(row > 0)
    def _():
        up.start()

    @pl.when(row == 0)
    def _():
        blocks[0] = jnp.zeros(blocks.shape[1:], BF)

    @pl.when(row == n_row - 1)
    def _():
        blocks[height // 16 + 1] = jnp.zeros(blocks.shape[1:], BF)

    @pl.when(row > 0)
    def _():
        copy(blocks.at[height // 16], blocks.at[0], s_row.at[0], r_row.at[0], {"row": lax.rem(row + n_row - 1, n_row)}).wait_recv()

    @pl.when(row < n_row - 1)
    def _():
        copy(blocks.at[1], blocks.at[height // 16 + 1], s_row.at[1], r_row.at[1], {"row": lax.rem(row + 1, n_row)}).wait_recv()

    def image_step(k, carry):
        pair = blocks[pl.ds(k, 2)].reshape(2 * bands * 16, 2 * LANES)
        out = mm(rows[...], pair).astype(BF)
        for pc in range(2):
            image[pl.ds(k * 8, 8), :, pc] = out[:, pc * LANES : (pc + 1) * LANES].reshape(8, 2, 16, LANES)
        return carry

    lax.fori_loop(0, height // 16 + 1, image_step, 0, unroll=True)

    def wide_rows(s):
        return jnp.concatenate(
            [image[pl.ds(s * STEP + r, 4)].reshape(256, LANES) for r in range(STEP)], axis=1
        )

    def forward_step(s, total):
        taps_out = mm(w_all[...], wide_rows(s))
        hid, mem = [], []
        for r in range(STEP):
            part_r = taps_out[:, r * LANES : (r + 1) * LANES]
            stem = part_r[:64]
            for b in range(1, 4):
                stem += pltpu.roll(part_r[64 * b : 64 * b + 64], LANES - b, 1)
            hid.append(jnp.maximum(stem, 0.0).astype(BF))
            mem.append(jnp.where(gids[pl.ds(s * STEP + r, 1), :] == key_ids, 1.0, 0.0).astype(BF))
        hid = jnp.concatenate(hid, axis=1)
        mem = jnp.concatenate(mem, axis=1)
        hidden[s] = hid
        member[s] = mem
        return total + mm_nt(mem, jnp.concatenate([hid, jnp.ones_like(hid)], axis=0))

    sums = lax.fori_loop(0, fr // STEP, forward_step, jnp.zeros((anchors, LANES), F32))
    counts = sums[:, 64:]
    pooled = sums[:, :64] / counts
    head = w_head[...]
    project = mm_high(pooled, head)
    length = jnp.sqrt(jnp.sum(project * project, axis=1, keepdims=True) + EPS)
    embed = project / length
    short = pooled / length
    keys[pl.ds(date, 1)] = fold(short).astype(keys.dtype)[None]
    key_sends = [copy(keys.at[date], keys.at[date], s_key.at[o], r_key.at[date], dev) for o, dev in peers]
    for c in key_sends:
        c.start()
    back = mm_nt(embed, head, HIGH)
    for o, dev in peers:
        copy(negs.at[o], negs.at[o], s_neg.at[o], r_neg.at[o], dev).wait_recv()
    target = key_date[date]
    source = 0
    for d in range(dates):
        source = jnp.where(key_date[d] == date, d, source)
    count_s[...] = count_keys(negs[source])
    for o, dev in peers:
        copy(keys.at[o], keys.at[o], s_key.at[o], r_key.at[o], dev).wait_recv()
    key_short = unfold(keys[target].astype(F32))
    own_short = unfold(keys[source].astype(F32))
    same = lax.broadcasted_iota(jnp.int32, (anchors, anchors), 0) == lax.broadcasted_iota(
        jnp.int32, (anchors, anchors), 1
    )
    scale = 1.0 / math.sqrt(dates * anchors * n_mem)

    def contrast(scores, count):
        positive = jnp.sum(jnp.where(same, scores, 0.0), axis=0, keepdims=True)
        weights = count * jnp.exp(scores)
        exp_pos = jnp.exp(positive)
        denominator = exp_pos + jnp.sum(weights, axis=0, keepdims=True)
        d_scores = (scale / TEMP) * (
            weights / denominator + jnp.where(same, exp_pos / denominator - 1.0, 0.0)
        )
        return d_scores, jnp.log(denominator) - positive

    d_scores, losses = contrast(mm_nt(key_short, back, HIGH) / TEMP, count_t[...])
    d_source, _ = contrast(mm_nt(back, own_short, HIGH) / TEMP, count_s[...])
    grad_short = mm_tn(d_scores, key_short, HIGH) + mm_high(d_source, own_short)
    n_down, n_across = fr // CELL, fc // CELL
    wide = n_across * tiles
    spot = lax.broadcasted_iota(jnp.int32, (wide, anchors), 1)
    pick = jnp.where(lax.rem(spot, wide) == lax.broadcasted_iota(jnp.int32, (wide, anchors), 0), losses, 0.0)
    line = lax.broadcasted_iota(jnp.int32, (n_down, anchors), 1) // wide
    lines = (line == lax.broadcasted_iota(jnp.int32, (n_down, anchors), 0)).astype(F32)
    loss_out[...] = mm_nt(pick, lines, HIGH).reshape(n_across, tiles, n_down)
    grad_embed = mm_high(grad_short, head)
    grad_project = (
        grad_embed - embed * jnp.sum(embed * grad_embed, axis=1, keepdims=True)
    ) / length
    head_term = mm_tn(pooled, grad_project, HIGH)
    hr, gr = 64 // n_row, 256 // n_row
    h_own[...] = head_term
    h_part[...] = head_term.astype(BF).reshape(n_row, hr, LANES)

    def give(src, dst, send, recv, me, group):
        return [copy(src(o), dst.at[me], send.at[o], recv.at[me], dev) for o, dev in group]

    def take(dst, send, recv, group):
        for o, dev in group:
            copy(dst.at[o], dst.at[o], send.at[o], recv.at[o], dev).wait_recv()

    def start(copies):
        for c in copies:
            c.start()
        return copies

    sends += key_sends + start(give(lambda o: h_part.at[o], h_got_1, s_h1, r_h1, row, rows_of))
    per_cell = (mm_nt(grad_project, head, HIGH) / counts).astype(BF)
    eye_c = (
        lax.broadcasted_iota(jnp.int32, (64, 64), 0) == lax.broadcasted_iota(jnp.int32, (64, 64), 1)
    ).astype(F32).astype(BF)
    cell_t = mm_nt(eye_c, per_cell).astype(BF)

    g_acc[...] = jnp.zeros_like(g_acc)

    def backward_step(s, carry):
        spread = mm(cell_t, member[s])
        slope = jnp.where(hidden[s].astype(F32) > 0.0, spread, 0.0)
        moved = [slope.astype(BF)]
        for b in range(1, 4):
            moved.append(
                jnp.concatenate(
                    [pltpu.roll(slope[:, r * LANES : (r + 1) * LANES], b, 1) for r in range(STEP)],
                    axis=1,
                ).astype(BF)
            )
        g_acc[...] += mm_nt(jnp.concatenate(moved, axis=0), wide_rows(s))
        return carry

    lax.fori_loop(0, fr // STEP, backward_step, 0)

    part[...] = g_acc[...].astype(BF).reshape(n_row, gr, 256)
    sends += start(give(lambda o: part.at[o], got_1, s_1, r_1, row, rows_of))

    def total_of(got, count):
        total = got[0].astype(F32)
        for m in range(1, count):
            total += got[m].astype(F32)
        return total.astype(BF)[None]

    def sum_rows(own, got, send, recv):
        take(got, send, recv, rows_of)
        total = own
        for o, _ in rows_of:
            total += got[pl.ds(o, 1)].reshape(own.shape).astype(F32)
        return total.astype(BF)[None]

    h_got_2[pl.ds(col, 1)] = sum_rows(h_own[pl.ds(row * hr, hr)], h_got_1, s_h1, r_h1)
    sends += start(give(lambda o: h_got_2.at[col], h_got_2, s_h2, r_h2, col, cols_of))
    got_2[pl.ds(col, 1)] = sum_rows(g_acc[pl.ds(row * gr, gr)], got_1, s_1, r_1)
    sends += start(give(lambda o: got_2.at[col], got_2, s_2, r_2, col, cols_of))
    take(h_got_2, s_h2, r_h2, cols_of)
    h_got_3[pl.ds(date, 1)] = total_of(h_got_2, n_col)
    sends += start(give(lambda o: h_got_3.at[date], h_got_3, s_h3, r_h3, date, peers))
    take(got_2, s_2, r_2, cols_of)
    got_3[pl.ds(date, 1)] = total_of(got_2, n_col)
    sends += start(give(lambda o: got_3.at[date], got_3, s_3, r_3, date, peers))
    take(h_got_3, s_h3, r_h3, peers)
    h_got_4[pl.ds(row, 1)] = total_of(h_got_3, dates)
    sends += start(give(lambda o: h_got_4.at[row], h_got_4, s_h4, r_h4, row, rows_of))
    take(got_3, s_3, r_3, peers)
    got_4[pl.ds(row, 1)] = total_of(got_3, dates)
    sends += start(give(lambda o: got_4.at[row], got_4, s_4, r_4, row, rows_of))
    take(h_got_4, s_h4, r_h4, rows_of)
    head_out[...] = h_got_4[...].reshape(64, LANES)
    take(got_4, s_4, r_4, rows_of)
    stem_out[...] = got_4[...].reshape(256, 256)

    for c in sends:
        c.wait_send()

    @pl.when(col < n_col - 1)
    def _():
        to_right.wait_send()

    @pl.when(col > 0)
    def _():
        to_left.wait_send()

    @pl.when(row < n_row - 1)
    def _():
        down.wait_send()

    @pl.when(row > 0)
    def _():
        up.wait_send()


def finish(loss, stem, head, taps, loss_out, stem_out, head_out):
    loss_out[...] = loss[...]
    head_out[...] = head[...].astype(F32)
    bands = stem_out.shape[0]
    result = jnp.zeros((bands * 56, 64), F32)
    for b in range(4):
        result += mm_nt(taps[b], stem[64 * b : 64 * b + 64])
    stem_out[...] = result.reshape(bands, 7, 8, 64)[:, :, :7, :]


def solution(mesh):
    n_row, n_col, dates = mesh.shape["row"], mesh.shape["col"], mesh.shape["date"]

    def local(pixels, w_stem, w_head, pool_grid, neg_index, key_date):
        _, tiles, bands, height, width = pixels.shape
        fr, fc = height // 2, width // 2
        cells = fr // CELL * (fc // CELL)
        anchors = tiles * cells
        w_taps = jnp.transpose(w_stem, (1, 2, 3, 0))
        grid_t = pool_grid.T
        neg = jnp.transpose(neg_index[0], (1, 2, 0, 3)).reshape(anchors, -1)
        place = np.zeros((fc, LANES), np.float32)
        for j in range(fc):
            for t in range(tiles):
                place[j, t * HALF + j] = 1
        vmem = pl.BlockSpec(memory_space=pltpu.VMEM)
        dma = pltpu.SemaphoreType.DMA
        cols, edge, halo, rows, taps = tables(tiles, bands, height, width)
        operands = (
            pixels[0], edge, w_taps, taps, grid_t, jnp.asarray(place, BF), neg, cols, halo, rows,
            w_head, key_date,
        )
        operands = [pltpu.with_memory_space_constraint(x, pltpu.HBM) for x in operands]
        loss, stem, head = pl.pallas_call(
            functools.partial(kernel, (tiles, bands, height, width, n_row, n_col, dates)),
            out_shape=(
                jax.ShapeDtypeStruct((fc // CELL, tiles, fr // CELL), F32),
                jax.ShapeDtypeStruct((256, 256), BF),
                jax.ShapeDtypeStruct((64, LANES), BF),
            ),
            in_specs=[pl.BlockSpec(memory_space=pltpu.HBM)] * len(operands),
            out_specs=(vmem, vmem, vmem),
            scratch_shapes=[pltpu.VMEM(x.shape, x.dtype) for x in operands[:-1]]
            + [pltpu.SMEM(key_date.shape, key_date.dtype)]
            + [
                pltpu.VMEM((2, bands, 16, height), BF),
                pltpu.VMEM((2, bands, 16, height), BF),
                pltpu.VMEM((height // 16 + 2, bands, 16, 2 * LANES), BF),
                pltpu.VMEM((height // 2 + 8, 2, 2, 16, LANES), BF),
                pltpu.VMEM((256, 256), BF),
                pltpu.VMEM((fr, LANES), F32),
                pltpu.VMEM((neg.shape[1], anchors), F32),
                pltpu.VMEM((anchors, anchors), F32),
                pltpu.VMEM((anchors, anchors), F32),
                pltpu.VMEM((dates, *neg.shape), BF),
                pltpu.VMEM((fr // STEP, anchors, STEP * LANES), BF),
                pltpu.VMEM((fr // STEP, 64, STEP * LANES), BF),
                pltpu.VMEM((dates, anchors // 2, LANES), KEY),
                pltpu.VMEM((256, 256), F32),
                pltpu.VMEM((n_row, 256 // n_row, 256), BF),
                pltpu.VMEM((n_row, 256 // n_row, 256), BF),
                pltpu.VMEM((n_col, 256 // n_row, 256), BF),
                pltpu.VMEM((dates, 256 // n_row, 256), BF),
                pltpu.VMEM((n_row, 256 // n_row, 256), BF),
                pltpu.VMEM((64, LANES), F32),
                pltpu.VMEM((n_row, 64 // n_row, LANES), BF),
                pltpu.VMEM((n_row, 64 // n_row, LANES), BF),
                pltpu.VMEM((n_col, 64 // n_row, LANES), BF),
                pltpu.VMEM((dates, 64 // n_row, LANES), BF),
                pltpu.VMEM((n_row, 64 // n_row, LANES), BF),
                dma((2,)), dma((2,)), dma((2,)), dma((2,)),
                dma((dates,)), dma((dates,)), dma((dates,)), dma((dates,)),
            ]
            + [dma((n,)) for n in (n_row, n_row, n_col, n_col, dates, dates, n_row, n_row)] * 2
            + [dma((len(operands),))],
            compiler_params=pltpu.CompilerParams(
                collective_id=0, has_side_effects=True, vmem_limit_bytes=32 * 2**20
            ),
        )(*operands)
        loss, stem, head = pl.pallas_call(
            finish,
            out_shape=(
                jax.ShapeDtypeStruct(loss.shape, F32),
                jax.ShapeDtypeStruct((bands, 7, 7, 64), F32),
                jax.ShapeDtypeStruct((64, LANES), F32),
            ),
            in_specs=[vmem] * 4,
            out_specs=(vmem, vmem, vmem),
            compiler_params=pltpu.CompilerParams(vmem_limit_bytes=8 * 2**20),
        )(loss, stem, head, taps)
        loss = loss.transpose(1, 2, 0)[None]
        return loss, jnp.transpose(stem, (3, 0, 1, 2)), head

    return jax.shard_map(
        local,
        mesh=mesh,
        in_specs=(
            P(("groups", "date"), None, None, "row", "col"),
            P(),
            P(),
            P("row", "col"),
            P(("groups", "date"), None, "row", "col", None),
            P(),
        ),
        out_specs=(
            P(("groups", "date"), None, "row", "col"),
            P("groups", None, None, None),
            P("groups", None),
        ),
        check_vma=False,
    )
```

```python
import functools
import math

import jax
import jax.numpy as jnp
import numpy as np
from jax import lax
from jax.experimental import pallas as pl
from jax.experimental.pallas import tpu as pltpu
from jax.sharding import PartitionSpec as P

CELL = 8
TEMP = 0.2
EPS = 1e-06
STEP = 24
LANES = 128
HALF = 64

MESH = pl.DeviceIdType.MESH
HIGH = lax.Precision.HIGHEST
BF = jnp.bfloat16
F32 = jnp.float32


def mm(left, right):
    return lax.dot_general(left, right, (((1,), (0,)), ((), ())), preferred_element_type=F32)


def mm_high(left, right):
    return lax.dot_general(
        left, right, (((1,), (0,)), ((), ())), precision=HIGH, preferred_element_type=F32
    )


def fold(array):
    half = array.shape[0] // 2
    return jnp.concatenate([array[:half], array[half:]], axis=1)


def unfold(array):
    half = array.shape[1] // 2
    return jnp.concatenate([array[:, :half], array[:, half:]], axis=0)


def mm_nt(left, right, precision=None):
    return lax.dot_general(
        left, right, (((1,), (1,)), ((), ())), precision=precision, preferred_element_type=F32
    )


def mm_tn(left, right, precision=None):
    return lax.dot_general(
        left, right, (((0,), (0,)), ((), ())), precision=precision, preferred_element_type=F32
    )


def tables(tiles, bands, height, width):
    cols = np.zeros((tiles * LANES, 2 * LANES), np.float32)
    edge = np.zeros((2, 32, tiles * LANES), np.float32)
    halo = np.zeros((32, 2, 2 * LANES), np.float32)
    for t in range(tiles):
        for w in range(width):
            q = w + 3
            cols[t * LANES + w, (q % 2) * LANES + t * HALF + q // 2] = 1
        for k in range(3):
            for p in range(2):
                spot = p * 8 + t * 3 + k
                edge[p, spot, t * LANES + width - 3 + k] = 1
                edge[p, 16 + spot, t * LANES + k] = 1
                halo[spot, p, (k % 2) * LANES + t * HALF + k // 2] = 1
                q = width + 3 + k
                halo[16 + spot, p, (q % 2) * LANES + t * HALF + q // 2] = 1
    rows = np.zeros((16, 16, bands, 16), np.float32)
    for r in range(16):
        for c in range(bands):
            rows[r, c, c, r] = 1
    taps = np.zeros((4, bands, 7, 8, 8, 2, 16), np.float32)
    for b in range(4):
        for c in range(bands):
            for u in range(7):
                for pc in range(2):
                    if 2 * b + pc < 7:
                        taps[b, c, u, 2 * b + pc, u, pc, c] = 1
    tables = (
        cols, edge, halo.reshape(32, 4 * LANES), rows.reshape(256, bands * 16), taps.reshape(4, bands * 56, 256),
    )
    return [jnp.asarray(x, BF) for x in tables]


def kernel(
    sizes,
    *refs,
):
    n_in = 12
    sources, outs = refs[:n_in], refs[n_in : n_in + 2]
    held, rest = refs[n_in + 2 : 2 * n_in + 2], refs[2 * n_in + 2 :]
    body(sizes, sources, held, *outs, *held, *rest)


def body(
    sizes, sources, held, loss_out, stem_out,
    pix, edge, w_taps, taps, grid_t, place, neg, cols, halo, rows, w_head, key_date,
    both_pix, pack, strips, blocks, image, w_all, gids, neg_t, count_t, count_s, negs, member, hidden,
    keys, g_head, g_acc, part, got_1, part_2, got_2, got_4,
    s_col, r_col, s_row, r_row, s_key, r_key, s_neg, r_neg, s_1, r_1, s_2, r_2, s_3, r_3, s_4, r_4,
    s_in,
):
    tiles, bands, height, width, n_row, n_col, dates = sizes
    fr, fc = height // 2, width // 2
    cells = fr // CELL * (fc // CELL)
    anchors = tiles * cells
    n_mem = n_row * n_col
    row, col, date = lax.axis_index("row"), lax.axis_index("col"), lax.axis_index("date")

    fetches = [pltpu.make_async_copy(a, b, s_in.at[i]) for i, (a, b) in enumerate(zip(sources, held))]
    for c in fetches:
        c.start()
    barrier = pltpu.get_barrier_semaphore()

    def others(name, count, mine):
        found = []
        for k in range(1, count):
            other = lax.rem(mine + k, count)
            found.append((other, {name: other}))
        return found

    rows_of, peers = others("row", n_row, row), others("date", dates, date)
    n_chip = n_col * dates
    chip = col * dates + date
    chips = []
    for k in range(1, n_chip):
        other = lax.rem(chip + k, n_chip)
        chips.append((other, {"col": other // dates, "date": lax.rem(other, dates)}))
    for _, dev in rows_of + chips:
        pl.semaphore_signal(barrier, inc=1, device_id=dev, device_id_type=MESH)

    fetches[0].wait()
    fetches[1].wait()

    for c in range(bands):
        flat = []
        for t in range(tiles):
            flat += [pix[t, c], jnp.zeros((height, LANES - width), BF)]
        both_pix[c] = jnp.concatenate(flat, axis=1)
    for g in range((bands + 1) // 2):
        ends = mm_nt(edge[0], both_pix[2 * g]).astype(BF)
        if 2 * g + 1 < bands:
            ends += mm_nt(edge[1], both_pix[2 * g + 1]).astype(BF)
        pack[0, g] = ends[:16]
        pack[1, g] = ends[16:]

    pl.semaphore_wait(barrier, len(rows_of) + len(chips))

    def copy(src, dst, send, recv, dev):
        return pltpu.make_async_remote_copy(
            src_ref=src, dst_ref=dst, send_sem=send, recv_sem=recv,
            device_id=dev, device_id_type=MESH,
        )

    to_right = copy(pack.at[0], strips.at[0], s_col.at[0], r_col.at[0], {"col": lax.rem(col + 1, n_col)})
    to_left = copy(pack.at[1], strips.at[1], s_col.at[1], r_col.at[1], {"col": lax.rem(col + n_col - 1, n_col)})
    down = copy(image.at[pl.ds(height, 3)], image.at[pl.ds(0, 3)], s_row.at[0], r_row.at[0], {"row": lax.rem(row + 1, n_row)})
    up = copy(image.at[pl.ds(3, 3)], image.at[pl.ds(height + 3, 3)], s_row.at[1], r_row.at[1], {"row": lax.rem(row + n_row - 1, n_row)})

    @pl.when(col < n_col - 1)
    def _():
        to_right.start()

    @pl.when(col > 0)
    def _():
        to_left.start()

    @pl.when(col == 0)
    def _():
        strips[0] = jnp.zeros(strips.shape[1:], BF)

    @pl.when(col == n_col - 1)
    def _():
        strips[1] = jnp.zeros(strips.shape[1:], BF)

    for c in fetches[2:]:
        c.wait()
    negs[pl.ds(date, 1)] = neg[...].astype(F32).astype(BF)[None]
    sends = [copy(negs.at[date], negs.at[date], s_neg.at[o], r_neg.at[date], dev) for o, dev in peers]
    for c in sends:
        c.start()

    for c in range(bands):
        wide = mm(both_pix[c], cols[...]).astype(BF)
        blocks[:, c] = wide.reshape(height // 16, 16, 2 * LANES)

    w_flat = w_taps[...].astype(F32)
    w_flat = jnp.concatenate([w_flat, jnp.zeros((bands, 7, 1, 64), F32)], axis=2)
    w_flat = w_flat.reshape(bands * 56, 64).astype(BF)
    for b in range(4):
        w_all[64 * b : 64 * b + 64, :] = mm_tn(w_flat, taps[b]).astype(BF)
    lane = lax.broadcasted_iota(jnp.int32, (1, LANES), 1)
    inside = lax.rem(lane, HALF) < fc
    shift = jnp.where(inside, (lane // HALF) * cells, -1000).astype(F32)
    gids[...] = mm_tn(grid_t[...].astype(F32).astype(BF), place[...]) + shift
    sub = lax.broadcasted_iota(jnp.int32, (anchors, 1), 0)
    key_ids = (lax.rem(sub, tiles) * cells + sub // tiles).astype(F32)
    n_neg = neg.shape[1]
    rest = anchors - LANES
    split = LANES // rest
    per = n_neg // split

    def at(axis, shape):
        return lax.broadcasted_iota(jnp.int32, shape, axis)

    def ones_at(mask):
        return mask.astype(F32).astype(BF)

    square = (n_neg, n_neg)
    eye_n = ones_at(at(0, square) == at(1, square))
    fold_n = ones_at(at(0, (per, n_neg)) == lax.rem(at(1, (per, n_neg)), per))
    in_group = at(0, (LANES, n_neg)) // rest == at(1, (LANES, n_neg)) // per
    regroup = ones_at(lax.rem(at(0, (LANES, rest)), rest) == at(1, (LANES, rest)))

    def count_keys(index):
        neg_t[:n_neg] = mm_nt(eye_n, index[:LANES])
        tail = jnp.where(in_group, jnp.concatenate([index[LANES:].astype(F32)] * split, axis=0), 0.0)
        neg_t[n_neg:] = mm_nt(fold_n, tail.astype(BF))

        def count_step(s, total):
            for k in range(8):
                total += jnp.where(neg_t[pl.ds(s * 8 + k, 1), :] == key_ids, 1.0, 0.0)
            return total

        first = lax.fori_loop(0, n_neg // 8, count_step, jnp.zeros((anchors, LANES), F32))
        last = lax.fori_loop(n_neg // 8, (n_neg + per) // 8, count_step, jnp.zeros((anchors, LANES), F32))
        return jnp.concatenate([first, mm(last.astype(BF), regroup)], axis=1)

    count_t[...] = count_keys(negs[date])

    @pl.when(col > 0)
    def _():
        copy(pack.at[0], strips.at[0], s_col.at[0], r_col.at[0], {"col": lax.rem(col + n_col - 1, n_col)}).wait_recv()

    @pl.when(col < n_col - 1)
    def _():
        copy(pack.at[1], strips.at[1], s_col.at[1], r_col.at[1], {"col": lax.rem(col + 1, n_col)}).wait_recv()

    for g in range((bands + 1) // 2):
        ends = mm_tn(jnp.concatenate([strips[0, g], strips[1, g]], axis=0), halo[...]).astype(BF)
        for p in range(min(2, bands - 2 * g)):
            wide = ends[:, 2 * LANES * p : 2 * LANES * (p + 1)].reshape(height // 16, 16, 2 * LANES)
            blocks[:, 2 * g + p] += wide

    def image_step(k):
        out = mm(rows[...], blocks[k].reshape(bands * 16, 2 * LANES)).astype(BF)
        for pc in range(2):
            image[pl.ds(16 * k + 3, 16), pc] = out[:, pc * LANES : (pc + 1) * LANES].reshape(16, 16, LANES)

    image_step(height // 16 - 1)
    image_step(0)

    @pl.when(row < n_row - 1)
    def _():
        down.start()

    @pl.when(row > 0)
    def _():
        up.start()

    @pl.when(row == 0)
    def _():
        image[:3] = jnp.zeros((3, *image.shape[1:]), BF)

    @pl.when(row == n_row - 1)
    def _():
        image[height + 3 :] = jnp.zeros((3, *image.shape[1:]), BF)

    for k in range(1, height // 16 - 1):
        image_step(k)

    @pl.when(row > 0)
    def _():
        copy(image.at[pl.ds(height, 3)], image.at[pl.ds(0, 3)], s_row.at[0], r_row.at[0], {"row": lax.rem(row + n_row - 1, n_row)}).wait_recv()

    @pl.when(row < n_row - 1)
    def _():
        copy(image.at[pl.ds(3, 3)], image.at[pl.ds(height + 3, 3)], s_row.at[1], r_row.at[1], {"row": lax.rem(row + 1, n_row)}).wait_recv()

    def wide_rows(s):
        return jnp.concatenate(
            [image[pl.ds(2 * (s * STEP + r), 8)].reshape(256, LANES) for r in range(STEP)], axis=1
        )

    def forward_step(s, total):
        taps_out = mm(w_all[...], wide_rows(s))
        hid, mem = [], []
        for r in range(STEP):
            part_r = taps_out[:, r * LANES : (r + 1) * LANES]
            stem = part_r[:64]
            for b in range(1, 4):
                stem += pltpu.roll(part_r[64 * b : 64 * b + 64], LANES - b, 1)
            hid.append(jnp.maximum(stem, 0.0).astype(BF))
            mem.append(jnp.where(gids[pl.ds(s * STEP + r, 1), :] == key_ids, 1.0, 0.0).astype(BF))
        hid = jnp.concatenate(hid, axis=1)
        mem = jnp.concatenate(mem, axis=1)
        hidden[s] = hid
        member[s] = mem
        return total + mm_nt(mem, jnp.concatenate([hid, jnp.ones_like(hid)], axis=0))

    sums = lax.fori_loop(0, fr // STEP, forward_step, jnp.zeros((anchors, LANES), F32))
    counts = sums[:, 64:]
    pooled = sums[:, :64] / counts
    head = w_head[...]
    project = mm_high(pooled, head)
    length = jnp.sqrt(jnp.sum(project * project, axis=1, keepdims=True) + EPS)
    embed = project / length
    short = pooled / length
    folded = fold(short)
    mean = jnp.mean(folded, axis=0, keepdims=True)
    away = folded - mean
    base = [away]
    for _ in range(3):
        term = mean.astype(BF).astype(F32)
        base.append(term)
        mean = mean - term
    base.append(jnp.zeros((5, LANES), F32))
    keys[pl.ds(date, 1)] = jnp.concatenate(base, axis=0).astype(BF)[None]
    key_sends = [copy(keys.at[date], keys.at[date], s_key.at[o], r_key.at[date], dev) for o, dev in peers]
    for c in key_sends:
        c.start()
    back = mm_nt(embed, head, HIGH)
    for o, dev in peers:
        copy(negs.at[o], negs.at[o], s_neg.at[o], r_neg.at[o], dev).wait_recv()
    target = key_date[date]
    source = 0
    for d in range(dates):
        source = jnp.where(key_date[d] == date, d, source)
    count_s[...] = count_keys(negs[source])
    for o, dev in peers:
        copy(keys.at[o], keys.at[o], s_key.at[o], r_key.at[o], dev).wait_recv()
    key_rows = anchors // 2

    def received(d):
        whole = keys[d].astype(F32)
        mean = whole[key_rows : key_rows + 1] + whole[key_rows + 1 : key_rows + 2] + whole[key_rows + 2 : key_rows + 3]
        return unfold(whole[:key_rows] + mean)

    key_short, own_short = received(target), received(source)
    same = lax.broadcasted_iota(jnp.int32, (anchors, anchors), 0) == lax.broadcasted_iota(
        jnp.int32, (anchors, anchors), 1
    )
    scale = 1.0 / math.sqrt(dates * anchors * n_mem)

    def contrast(scores, count):
        positive = jnp.sum(jnp.where(same, scores, 0.0), axis=0, keepdims=True)
        weights = count * jnp.exp(scores)
        exp_pos = jnp.exp(positive)
        denominator = exp_pos + jnp.sum(weights, axis=0, keepdims=True)
        d_scores = (scale / TEMP) * (
            weights / denominator + jnp.where(same, exp_pos / denominator - 1.0, 0.0)
        )
        return d_scores, jnp.log(denominator) - positive

    d_scores, losses = contrast(mm_nt(key_short, back, HIGH) / TEMP, count_t[...])
    d_source, _ = contrast(mm_nt(back, own_short, HIGH) / TEMP, count_s[...])
    grad_short = mm_tn(d_scores, key_short, HIGH) + mm_high(d_source, own_short)
    n_down, n_across = fr // CELL, fc // CELL
    wide = n_across * tiles
    spot = lax.broadcasted_iota(jnp.int32, (wide, anchors), 1)
    pick = jnp.where(lax.rem(spot, wide) == lax.broadcasted_iota(jnp.int32, (wide, anchors), 0), losses, 0.0)
    line = lax.broadcasted_iota(jnp.int32, (n_down, anchors), 1) // wide
    lines = (line == lax.broadcasted_iota(jnp.int32, (n_down, anchors), 0)).astype(F32)
    loss_out[...] = mm_nt(pick, lines, HIGH).reshape(n_across, tiles, n_down)
    grad_embed = mm_high(grad_short, head)
    grad_project = (
        grad_embed - embed * jnp.sum(embed * grad_embed, axis=1, keepdims=True)
    ) / length
    head_term = mm_tn(pooled, grad_project, HIGH)
    sends += key_sends
    g_head[...] = head_term
    per_cell = (mm_nt(grad_project, head, HIGH) / counts).astype(BF)
    eye_c = (
        lax.broadcasted_iota(jnp.int32, (64, 64), 0) == lax.broadcasted_iota(jnp.int32, (64, 64), 1)
    ).astype(F32).astype(BF)
    cell_t = mm_nt(eye_c, per_cell).astype(BF)

    g_acc[...] = jnp.zeros_like(g_acc)

    def backward_step(s, carry):
        spread = mm(cell_t, member[s])
        slope = jnp.where(hidden[s].astype(F32) > 0.0, spread, 0.0)
        moved = [slope.astype(BF)]
        for b in range(1, 4):
            moved.append(
                jnp.concatenate(
                    [pltpu.roll(slope[:, r * LANES : (r + 1) * LANES], b, 1) for r in range(STEP)],
                    axis=1,
                ).astype(BF)
            )
        g_acc[...] += mm_nt(wide_rows(s), jnp.concatenate(moved, axis=0))
        return carry

    lax.fori_loop(0, fr // STEP, backward_step, 0)

    g_acc[224:, :LANES] = g_head[:32]
    g_acc[224:, LANES:] = g_head[32:]
    gr = 256 // n_row
    owners = min(n_chip, gr // 16)
    every = owners == n_chip
    part[...] = g_acc[...].astype(BF).reshape(n_row, gr, 256)
    step_1 = [copy(part.at[o], got_1.at[row], s_1.at[o], r_1.at[row], dev) for o, dev in rows_of]
    for c in step_1:
        c.start()

    def when(chosen, run):
        if every:
            run()
        else:
            pl.when(chosen)(run)

    total = g_acc[pl.ds(row * gr, gr)]
    for o, dev in rows_of:
        copy(part.at[o], got_1.at[o], s_1.at[o], r_1.at[o], dev).wait_recv()
        total += got_1[pl.ds(o, 1)].reshape(gr, 256).astype(F32)
    part_2[...] = total.astype(BF).reshape(part_2.shape)
    step_2 = [copy(part_2.at[o], got_2.at[chip], s_2.at[o], r_2.at[chip], dev) for o, dev in chips]
    for (o, _), c in zip(chips, step_2):
        when(o < owners, c.start)
    across = [copy(got_4.at[row, chip], got_4.at[row, chip], s_3.at[o], r_3.at[chip], dev) for o, dev in chips]

    def own_chunk():
        got_2[pl.ds(chip, 1)] = part_2[pl.ds(chip, 1)]
        for o, dev in chips:
            copy(got_2.at[o], got_2.at[o], s_2.at[o], r_2.at[o], dev).wait_recv()
        total = got_2[0].astype(F32)
        for m in range(1, n_chip):
            total += got_2[m].astype(F32)
        got_4[row, pl.ds(chip, 1)] = total.astype(BF)[None]
        for c in across:
            c.start()

    when(chip < owners, own_chunk)

    def pass_on(o):
        return [copy(got_4.at[row, o], got_4.at[row, o], s_4.at[k, o], r_4.at[row, o], dev) for k, dev in rows_of]

    def start_all(copies):
        for c in copies:
            c.start()

    when(chip < owners, lambda: start_all(pass_on(chip)))
    for o, dev in chips:
        def arrived(o=o, dev=dev):
            copy(got_4.at[row, o], got_4.at[row, o], s_3.at[o], r_3.at[o], dev).wait_recv()
            start_all(pass_on(o))

        when(o < owners, arrived)
    for k, dev in rows_of:
        for o in range(owners):
            copy(got_4.at[k, o], got_4.at[k, o], s_4.at[k, o], r_4.at[k, o], dev).wait_recv()
    stem_out[...] = got_4[...].reshape(256, 256)

    for (o, _), c in zip(chips, step_2):
        when(o < owners, c.wait_send)
    when(chip < owners, lambda: [c.wait_send() for c in across] and None)
    for o in range(owners):
        for c in pass_on(o):
            c.wait_send()
    sends += step_1
    for c in sends:
        c.wait_send()

    @pl.when(col < n_col - 1)
    def _():
        to_right.wait_send()

    @pl.when(col > 0)
    def _():
        to_left.wait_send()

    @pl.when(row < n_row - 1)
    def _():
        down.wait_send()

    @pl.when(row > 0)
    def _():
        up.wait_send()


def finish(loss, stem, taps, loss_out, stem_out, head_out):
    loss_out[...] = loss[...]
    head_out[...] = unfold(stem[224:].astype(F32))
    bands = stem_out.shape[0]
    result = jnp.zeros((bands * 56, 64), F32)
    for b in range(4):
        result += mm(taps[b], stem[:, 64 * b : 64 * b + 64])
    stem_out[...] = result.reshape(bands, 7, 8, 64)[:, :, :7, :]


def solution(mesh):
    n_row, n_col, dates = mesh.shape["row"], mesh.shape["col"], mesh.shape["date"]

    def local(pixels, w_stem, w_head, pool_grid, neg_index, key_date):
        _, tiles, bands, height, width = pixels.shape
        fr, fc = height // 2, width // 2
        cells = fr // CELL * (fc // CELL)
        anchors = tiles * cells
        w_taps = jnp.transpose(w_stem, (1, 2, 3, 0))
        grid_t = pool_grid.T
        neg = jnp.transpose(neg_index[0], (1, 2, 0, 3)).reshape(anchors, -1)
        place = np.zeros((fc, LANES), np.float32)
        for j in range(fc):
            for t in range(tiles):
                place[j, t * HALF + j] = 1
        groups, half, n_chip = (bands + 1) // 2, 256 // n_row, n_col * dates
        owners = min(n_chip, half // 16)
        vmem = pl.BlockSpec(memory_space=pltpu.VMEM)
        dma = pltpu.SemaphoreType.DMA
        cols, edge, halo, rows, taps = tables(tiles, bands, height, width)
        operands = (
            pixels[0], edge, w_taps, taps, grid_t, jnp.asarray(place, BF), neg, cols, halo, rows,
            w_head, key_date,
        )
        operands = [pltpu.with_memory_space_constraint(x, pltpu.HBM) for x in operands]
        loss, stem = pl.pallas_call(
            functools.partial(kernel, (tiles, bands, height, width, n_row, n_col, dates)),
            out_shape=(
                jax.ShapeDtypeStruct((fc // CELL, tiles, fr // CELL), F32),
                jax.ShapeDtypeStruct((256, 256), BF),
            ),
            in_specs=[pl.BlockSpec(memory_space=pltpu.HBM)] * len(operands),
            out_specs=(vmem, vmem),
            scratch_shapes=[pltpu.VMEM(x.shape, x.dtype) for x in operands[:-1]]
            + [pltpu.SMEM(key_date.shape, key_date.dtype)]
            + [
                pltpu.VMEM((bands, height, tiles * LANES), BF),
                pltpu.VMEM((2, groups, 16, height), BF),
                pltpu.VMEM((2, groups, 16, height), BF),
                pltpu.VMEM((height // 16, bands, 16, 2 * LANES), BF),
                pltpu.VMEM((height + 6, 2, 16, LANES), BF),
                pltpu.VMEM((256, 256), BF),
                pltpu.VMEM((fr, LANES), F32),
                pltpu.VMEM((neg.shape[1] * anchors // LANES, LANES), F32),
                pltpu.VMEM((anchors, anchors), F32),
                pltpu.VMEM((anchors, anchors), F32),
                pltpu.VMEM((dates, *neg.shape), BF),
                pltpu.VMEM((fr // STEP, anchors, STEP * LANES), BF),
                pltpu.VMEM((fr // STEP, 64, STEP * LANES), BF),
                pltpu.VMEM((dates, anchors // 2 + 8, LANES), BF),
                pltpu.VMEM((64, LANES), F32),
                pltpu.VMEM((256, 256), F32),
                pltpu.VMEM((n_row, half, 256), BF),
                pltpu.VMEM((n_row, half, 256), BF),
                pltpu.VMEM((owners, half // owners, 256), BF),
                pltpu.VMEM((n_chip, half // owners, 256), BF),
                pltpu.VMEM((n_row, owners, half // owners, 256), BF),
                dma((2,)), dma((2,)), dma((2,)), dma((2,)),
                dma((dates,)), dma((dates,)), dma((dates,)), dma((dates,)),
                dma((n_row,)), dma((n_row,)), dma((n_chip,)), dma((n_chip,)), dma((n_chip,)), dma((n_chip,)),
                dma((n_row, owners)), dma((n_row, owners)), dma((len(operands),)),
            ],
            compiler_params=pltpu.CompilerParams(
                collective_id=0, has_side_effects=True, vmem_limit_bytes=32 * 2**20
            ),
        )(*operands)
        loss, stem, head = pl.pallas_call(
            finish,
            out_shape=(
                jax.ShapeDtypeStruct(loss.shape, F32),
                jax.ShapeDtypeStruct((bands, 7, 7, 64), F32),
                jax.ShapeDtypeStruct((64, LANES), F32),
            ),
            in_specs=[vmem] * 3,
            out_specs=(vmem, vmem, vmem),
            compiler_params=pltpu.CompilerParams(vmem_limit_bytes=8 * 2**20),
        )(loss, stem, taps)
        loss = loss.transpose(1, 2, 0)[None]
        return loss, jnp.transpose(stem, (3, 0, 1, 2)), head

    return jax.shard_map(
        local,
        mesh=mesh,
        in_specs=(
            P(("groups", "date"), None, None, "row", "col"),
            P(),
            P(),
            P("row", "col"),
            P(("groups", "date"), None, "row", "col", None),
            P(),
        ),
        out_specs=(
            P(("groups", "date"), None, "row", "col"),
            P("groups", None, None, None),
            P("groups", None),
        ),
        check_vma=False,
    )
```

```python
import functools
import math

import jax
import jax.numpy as jnp
import numpy as np
from jax import lax
from jax.experimental import pallas as pl
from jax.experimental.pallas import tpu as pltpu
from jax.sharding import PartitionSpec as P

CELL = 8
TEMP = 0.2
EPS = 1e-06
STEP = 48
LANES = 128
HALF = 64

MESH = pl.DeviceIdType.MESH
HIGH = lax.Precision.HIGHEST
BF = jnp.bfloat16
F32 = jnp.float32


def mm(left, right):
    return lax.dot_general(left, right, (((1,), (0,)), ((), ())), preferred_element_type=F32)


def mm_high(left, right):
    return lax.dot_general(
        left, right, (((1,), (0,)), ((), ())), precision=HIGH, preferred_element_type=F32
    )


def fold(array):
    half = array.shape[0] // 2
    return jnp.concatenate([array[:half], array[half:]], axis=1)


def unfold(array):
    half = array.shape[1] // 2
    return jnp.concatenate([array[:, :half], array[:, half:]], axis=0)


def mm_nt(left, right, precision=None):
    return lax.dot_general(
        left, right, (((1,), (1,)), ((), ())), precision=precision, preferred_element_type=F32
    )


def mm_tn(left, right, precision=None):
    return lax.dot_general(
        left, right, (((0,), (0,)), ((), ())), precision=precision, preferred_element_type=F32
    )


def tables(tiles, bands, height, width):
    cols = np.zeros((tiles * LANES, 2 * LANES), np.float32)
    edge = np.zeros((2, 32, tiles * LANES), np.float32)
    halo = np.zeros((32, 2, 2 * LANES), np.float32)
    for t in range(tiles):
        for w in range(width):
            q = w + 3
            cols[t * LANES + w, (q % 2) * LANES + t * HALF + q // 2] = 1
        for k in range(3):
            for p in range(2):
                spot = p * 8 + t * 3 + k
                edge[p, spot, t * LANES + width - 3 + k] = 1
                edge[p, 16 + spot, t * LANES + k] = 1
                halo[spot, p, (k % 2) * LANES + t * HALF + k // 2] = 1
                q = width + 3 + k
                halo[16 + spot, p, (q % 2) * LANES + t * HALF + q // 2] = 1
    rows = np.zeros((16, 16, bands, 16), np.float32)
    for r in range(16):
        for c in range(bands):
            rows[r, c, c, r] = 1
    taps = np.zeros((4, bands, 7, 8, 8, 2, 16), np.float32)
    for b in range(4):
        for c in range(bands):
            for u in range(7):
                for pc in range(2):
                    if 2 * b + pc < 7:
                        taps[b, c, u, 2 * b + pc, u, pc, c] = 1
    tables = (
        cols, edge, halo.reshape(32, 4 * LANES), rows.reshape(256, bands * 16), taps.reshape(4, bands * 56, 256),
    )
    return [jnp.asarray(x, BF) for x in tables]


def kernel(
    sizes,
    *refs,
):
    n_in = 12
    sources, outs = refs[:n_in], refs[n_in : n_in + 2]
    held, rest = refs[n_in + 2 : 2 * n_in + 2], refs[2 * n_in + 2 :]
    body(sizes, sources, held, *outs, *held, *rest)


def body(
    sizes, sources, held, loss_out, stem_out,
    pix, edge, w_taps, taps, grid_t, place, neg, cols, halo, rows, w_head, key_date,
    both_pix, pack, strips, blocks, image, w_all, gids, neg_t, count_t, count_s, negs, member, hidden,
    keys, g_head, g_acc, part, got_1, part_2, got_2, got_4,
    s_col, r_col, s_row, r_row, s_key, r_key, s_neg, r_neg, s_1, r_1, s_2, r_2, s_3, r_3, s_4, r_4,
    s_in,
):
    tiles, bands, height, width, n_row, n_col, dates = sizes
    fr, fc = height // 2, width // 2
    cells = fr // CELL * (fc // CELL)
    anchors = tiles * cells
    n_mem = n_row * n_col
    row, col, date = lax.axis_index("row"), lax.axis_index("col"), lax.axis_index("date")

    fetches = [pltpu.make_async_copy(a, b, s_in.at[i]) for i, (a, b) in enumerate(zip(sources, held))]
    for c in fetches:
        c.start()
    barrier = pltpu.get_barrier_semaphore()

    def others(name, count, mine):
        found = []
        for k in range(1, count):
            other = lax.rem(mine + k, count)
            found.append((other, {name: other}))
        return found

    rows_of, peers = others("row", n_row, row), others("date", dates, date)
    n_chip = n_col * dates
    chip = col * dates + date
    chips = []
    for k in range(1, n_chip):
        other = lax.rem(chip + k, n_chip)
        chips.append((other, {"col": other // dates, "date": lax.rem(other, dates)}))
    for _, dev in rows_of + chips:
        pl.semaphore_signal(barrier, inc=1, device_id=dev, device_id_type=MESH)

    fetches[0].wait()
    fetches[1].wait()

    for c in range(bands):
        flat = []
        for t in range(tiles):
            flat += [pix[t, c], jnp.zeros((height, LANES - width), BF)]
        both_pix[c] = jnp.concatenate(flat, axis=1)
    for g in range((bands + 1) // 2):
        ends = mm_nt(edge[0], both_pix[2 * g]).astype(BF)
        if 2 * g + 1 < bands:
            ends += mm_nt(edge[1], both_pix[2 * g + 1]).astype(BF)
        pack[0, g] = ends[:16]
        pack[1, g] = ends[16:]

    pl.semaphore_wait(barrier, len(rows_of) + len(chips))

    def copy(src, dst, send, recv, dev):
        return pltpu.make_async_remote_copy(
            src_ref=src, dst_ref=dst, send_sem=send, recv_sem=recv,
            device_id=dev, device_id_type=MESH,
        )

    to_right = copy(pack.at[0], strips.at[0], s_col.at[0], r_col.at[0], {"col": lax.rem(col + 1, n_col)})
    to_left = copy(pack.at[1], strips.at[1], s_col.at[1], r_col.at[1], {"col": lax.rem(col + n_col - 1, n_col)})
    down = copy(image.at[pl.ds(height, 3)], image.at[pl.ds(0, 3)], s_row.at[0], r_row.at[0], {"row": lax.rem(row + 1, n_row)})
    up = copy(image.at[pl.ds(3, 3)], image.at[pl.ds(height + 3, 3)], s_row.at[1], r_row.at[1], {"row": lax.rem(row + n_row - 1, n_row)})

    @pl.when(col < n_col - 1)
    def _():
        to_right.start()

    @pl.when(col > 0)
    def _():
        to_left.start()

    @pl.when(col == 0)
    def _():
        strips[0] = jnp.zeros(strips.shape[1:], BF)

    @pl.when(col == n_col - 1)
    def _():
        strips[1] = jnp.zeros(strips.shape[1:], BF)

    for c in fetches[2:]:
        c.wait()
    negs[pl.ds(date, 1)] = neg[...].astype(F32).astype(BF)[None]
    sends = [copy(negs.at[date], negs.at[date], s_neg.at[o], r_neg.at[date], dev) for o, dev in peers]
    for c in sends:
        c.start()

    for c in range(bands):
        wide = mm(both_pix[c], cols[...]).astype(BF)
        blocks[:, c] = wide.reshape(height // 16, 16, 2 * LANES)

    w_flat = w_taps[...].astype(F32)
    w_flat = jnp.concatenate([w_flat, jnp.zeros((bands, 7, 1, 64), F32)], axis=2)
    w_flat = w_flat.reshape(bands * 56, 64).astype(BF)
    for b in range(4):
        w_all[64 * b : 64 * b + 64, :] = mm_tn(w_flat, taps[b]).astype(BF)
    lane = lax.broadcasted_iota(jnp.int32, (1, LANES), 1)
    inside = lax.rem(lane, HALF) < fc
    shift = jnp.where(inside, (lane // HALF) * cells, -1000).astype(F32)
    gids[...] = mm_tn(grid_t[...].astype(F32).astype(BF), place[...]) + shift
    sub = lax.broadcasted_iota(jnp.int32, (anchors, 1), 0)
    key_ids = (lax.rem(sub, tiles) * cells + sub // tiles).astype(F32)
    n_neg = neg.shape[1]
    rest = anchors - LANES
    split = LANES // rest
    per = n_neg // split

    def at(axis, shape):
        return lax.broadcasted_iota(jnp.int32, shape, axis)

    def ones_at(mask):
        return mask.astype(F32).astype(BF)

    square = (n_neg, n_neg)
    eye_n = ones_at(at(0, square) == at(1, square))
    fold_n = ones_at(at(0, (per, n_neg)) == lax.rem(at(1, (per, n_neg)), per))
    in_group = at(0, (LANES, n_neg)) // rest == at(1, (LANES, n_neg)) // per
    regroup = ones_at(lax.rem(at(0, (LANES, rest)), rest) == at(1, (LANES, rest)))

    def count_keys(index):
        neg_t[:n_neg] = mm_nt(eye_n, index[:LANES])
        tail = jnp.where(in_group, jnp.concatenate([index[LANES:].astype(F32)] * split, axis=0), 0.0)
        neg_t[n_neg:] = mm_nt(fold_n, tail.astype(BF))

        def count_step(s, total):
            for k in range(8):
                total += jnp.where(neg_t[pl.ds(s * 8 + k, 1), :] == key_ids, 1.0, 0.0)
            return total

        first = lax.fori_loop(0, n_neg // 8, count_step, jnp.zeros((anchors, LANES), F32))
        last = lax.fori_loop(n_neg // 8, (n_neg + per) // 8, count_step, jnp.zeros((anchors, LANES), F32))
        return jnp.concatenate([first, mm(last.astype(BF), regroup)], axis=1)

    count_t[...] = count_keys(negs[date])

    @pl.when(col > 0)
    def _():
        copy(pack.at[0], strips.at[0], s_col.at[0], r_col.at[0], {"col": lax.rem(col + n_col - 1, n_col)}).wait_recv()

    @pl.when(col < n_col - 1)
    def _():
        copy(pack.at[1], strips.at[1], s_col.at[1], r_col.at[1], {"col": lax.rem(col + 1, n_col)}).wait_recv()

    for g in range((bands + 1) // 2):
        ends = mm_tn(jnp.concatenate([strips[0, g], strips[1, g]], axis=0), halo[...]).astype(BF)
        for p in range(min(2, bands - 2 * g)):
            wide = ends[:, 2 * LANES * p : 2 * LANES * (p + 1)].reshape(height // 16, 16, 2 * LANES)
            blocks[:, 2 * g + p] += wide

    def image_step(k):
        out = mm(rows[...], blocks[k].reshape(bands * 16, 2 * LANES)).astype(BF)
        for pc in range(2):
            image[pl.ds(16 * k + 3, 16), pc] = out[:, pc * LANES : (pc + 1) * LANES].reshape(16, 16, LANES)

    image_step(height // 16 - 1)
    image_step(0)

    @pl.when(row < n_row - 1)
    def _():
        down.start()

    @pl.when(row > 0)
    def _():
        up.start()

    @pl.when(row == 0)
    def _():
        image[:3] = jnp.zeros((3, *image.shape[1:]), BF)

    @pl.when(row == n_row - 1)
    def _():
        image[height + 3 :] = jnp.zeros((3, *image.shape[1:]), BF)

    for k in range(1, height // 16 - 1):
        image_step(k)

    @pl.when(row > 0)
    def _():
        copy(image.at[pl.ds(height, 3)], image.at[pl.ds(0, 3)], s_row.at[0], r_row.at[0], {"row": lax.rem(row + n_row - 1, n_row)}).wait_recv()

    @pl.when(row < n_row - 1)
    def _():
        copy(image.at[pl.ds(3, 3)], image.at[pl.ds(height + 3, 3)], s_row.at[1], r_row.at[1], {"row": lax.rem(row + 1, n_row)}).wait_recv()

    def wide_rows(s):
        return jnp.concatenate(
            [image[pl.ds(2 * (s * STEP + r), 8)].reshape(256, LANES) for r in range(STEP)], axis=1
        )

    def forward_step(s, total):
        taps_out = mm(w_all[...], wide_rows(s))
        hid, mem = [], []
        for r in range(STEP):
            part_r = taps_out[:, r * LANES : (r + 1) * LANES]
            stem = part_r[:64]
            for b in range(1, 4):
                stem += pltpu.roll(part_r[64 * b : 64 * b + 64], LANES - b, 1)
            hid.append(jnp.maximum(stem, 0.0).astype(BF))
            mem.append(jnp.where(gids[pl.ds(s * STEP + r, 1), :] == key_ids, 1.0, 0.0).astype(BF))
        hid = jnp.concatenate(hid, axis=1)
        mem = jnp.concatenate(mem, axis=1)
        hidden[s] = hid
        member[s] = mem
        return total + mm_nt(mem, jnp.concatenate([hid, jnp.ones_like(hid)], axis=0))

    sums = lax.fori_loop(0, fr // STEP, forward_step, jnp.zeros((anchors, LANES), F32))
    counts = sums[:, 64:]
    pooled = sums[:, :64] / counts
    head = w_head[...]
    project = mm_high(pooled, head)
    length = jnp.sqrt(jnp.sum(project * project, axis=1, keepdims=True) + EPS)
    embed = project / length
    short = pooled / length
    folded = fold(short)
    mean = jnp.mean(folded, axis=0, keepdims=True)
    away = folded - mean
    base = [away]
    for _ in range(3):
        term = mean.astype(BF).astype(F32)
        base.append(term)
        mean = mean - term
    base.append(jnp.zeros((5, LANES), F32))
    keys[pl.ds(date, 1)] = jnp.concatenate(base, axis=0).astype(BF)[None]
    key_sends = [copy(keys.at[date], keys.at[date], s_key.at[o], r_key.at[date], dev) for o, dev in peers]
    for c in key_sends:
        c.start()
    back = mm_nt(embed, head, HIGH)
    for o, dev in peers:
        copy(negs.at[o], negs.at[o], s_neg.at[o], r_neg.at[o], dev).wait_recv()
    target = key_date[date]
    source = 0
    for d in range(dates):
        source = jnp.where(key_date[d] == date, d, source)
    count_s[...] = count_keys(negs[source])
    for o, dev in peers:
        copy(keys.at[o], keys.at[o], s_key.at[o], r_key.at[o], dev).wait_recv()
    key_rows = anchors // 2

    def received(d):
        whole = keys[d].astype(F32)
        mean = whole[key_rows : key_rows + 1] + whole[key_rows + 1 : key_rows + 2] + whole[key_rows + 2 : key_rows + 3]
        return unfold(whole[:key_rows] + mean)

    key_short, own_short = received(target), received(source)
    same = lax.broadcasted_iota(jnp.int32, (anchors, anchors), 0) == lax.broadcasted_iota(
        jnp.int32, (anchors, anchors), 1
    )
    scale = 1.0 / math.sqrt(dates * anchors * n_mem)

    def contrast(scores, count):
        positive = jnp.sum(jnp.where(same, scores, 0.0), axis=0, keepdims=True)
        weights = count * jnp.exp(scores)
        exp_pos = jnp.exp(positive)
        denominator = exp_pos + jnp.sum(weights, axis=0, keepdims=True)
        d_scores = (scale / TEMP) * (
            weights / denominator + jnp.where(same, exp_pos / denominator - 1.0, 0.0)
        )
        return d_scores, jnp.log(denominator) - positive

    d_scores, losses = contrast(mm_nt(key_short, back, HIGH) / TEMP, count_t[...])
    d_source, _ = contrast(mm_nt(back, own_short, HIGH) / TEMP, count_s[...])
    grad_short = mm_tn(d_scores, key_short, HIGH) + mm_high(d_source, own_short)
    n_down, n_across = fr // CELL, fc // CELL
    wide = n_across * tiles
    spot = lax.broadcasted_iota(jnp.int32, (wide, anchors), 1)
    pick = jnp.where(lax.rem(spot, wide) == lax.broadcasted_iota(jnp.int32, (wide, anchors), 0), losses, 0.0)
    line = lax.broadcasted_iota(jnp.int32, (n_down, anchors), 1) // wide
    lines = (line == lax.broadcasted_iota(jnp.int32, (n_down, anchors), 0)).astype(F32)
    loss_out[...] = mm_nt(pick, lines, HIGH).reshape(n_across, tiles, n_down)
    grad_embed = mm_high(grad_short, head)
    grad_project = (
        grad_embed - embed * jnp.sum(embed * grad_embed, axis=1, keepdims=True)
    ) / length
    head_term = mm_tn(pooled, grad_project, HIGH)
    sends += key_sends
    g_head[...] = head_term
    per_cell = (mm_nt(grad_project, head, HIGH) / counts).astype(BF)
    eye_c = (
        lax.broadcasted_iota(jnp.int32, (64, 64), 0) == lax.broadcasted_iota(jnp.int32, (64, 64), 1)
    ).astype(F32).astype(BF)
    cell_t = mm_nt(eye_c, per_cell).astype(BF)

    g_acc[...] = jnp.zeros_like(g_acc)

    def backward_step(s, carry):
        spread = mm(cell_t, member[s])
        slope = jnp.where(hidden[s] > 0, spread.astype(BF), jnp.zeros((), BF))
        moved = [slope]
        for b in range(1, 4):
            moved.append(
                jnp.concatenate(
                    [pltpu.roll(slope[:, r * LANES : (r + 1) * LANES], b, 1) for r in range(STEP)], axis=1
                )
            )
        g_acc[...] += mm_nt(wide_rows(s), jnp.concatenate(moved, axis=0))
        return carry

    lax.fori_loop(0, fr // STEP, backward_step, 0)

    g_acc[224:, :LANES] = g_head[:32]
    g_acc[224:, LANES:] = g_head[32:]
    gr = 256 // n_row
    owners = min(n_chip, gr // 16)
    every = owners == n_chip
    part[...] = g_acc[...].astype(BF).reshape(n_row, gr, 256)
    step_1 = [copy(part.at[o], got_1.at[row], s_1.at[o], r_1.at[row], dev) for o, dev in rows_of]
    for c in step_1:
        c.start()

    def when(chosen, run):
        if every:
            run()
        else:
            pl.when(chosen)(run)

    total = g_acc[pl.ds(row * gr, gr)]
    for o, dev in rows_of:
        copy(part.at[o], got_1.at[o], s_1.at[o], r_1.at[o], dev).wait_recv()
        total += got_1[pl.ds(o, 1)].reshape(gr, 256).astype(F32)
    part_2[...] = total.astype(BF).reshape(part_2.shape)
    step_2 = [copy(part_2.at[o], got_2.at[chip], s_2.at[o], r_2.at[chip], dev) for o, dev in chips]
    for (o, _), c in zip(chips, step_2):
        when(o < owners, c.start)
    across = [copy(got_4.at[row, chip], got_4.at[row, chip], s_3.at[o], r_3.at[chip], dev) for o, dev in chips]

    def own_chunk():
        got_2[pl.ds(chip, 1)] = part_2[pl.ds(chip, 1)]
        for o, dev in chips:
            copy(got_2.at[o], got_2.at[o], s_2.at[o], r_2.at[o], dev).wait_recv()
        total = got_2[0].astype(F32)
        for m in range(1, n_chip):
            total += got_2[m].astype(F32)
        got_4[row, pl.ds(chip, 1)] = total.astype(BF)[None]
        for c in across:
            c.start()

    when(chip < owners, own_chunk)

    def pass_on(o):
        return [copy(got_4.at[row, o], got_4.at[row, o], s_4.at[k, o], r_4.at[row, o], dev) for k, dev in rows_of]

    def start_all(copies):
        for c in copies:
            c.start()

    when(chip < owners, lambda: start_all(pass_on(chip)))
    for o, dev in chips:
        def arrived(o=o, dev=dev):
            copy(got_4.at[row, o], got_4.at[row, o], s_3.at[o], r_3.at[o], dev).wait_recv()
            start_all(pass_on(o))

        when(o < owners, arrived)
    for k, dev in rows_of:
        for o in range(owners):
            copy(got_4.at[k, o], got_4.at[k, o], s_4.at[k, o], r_4.at[k, o], dev).wait_recv()
    stem_out[...] = got_4[...].reshape(256, 256)

    for (o, _), c in zip(chips, step_2):
        when(o < owners, c.wait_send)
    when(chip < owners, lambda: [c.wait_send() for c in across] and None)
    for o in range(owners):
        for c in pass_on(o):
            c.wait_send()
    sends += step_1
    for c in sends:
        c.wait_send()

    @pl.when(col < n_col - 1)
    def _():
        to_right.wait_send()

    @pl.when(col > 0)
    def _():
        to_left.wait_send()

    @pl.when(row < n_row - 1)
    def _():
        down.wait_send()

    @pl.when(row > 0)
    def _():
        up.wait_send()


def finish(loss, stem, taps, loss_out, stem_out, head_out):
    loss_out[...] = loss[...]
    head_out[...] = unfold(stem[224:].astype(F32))
    bands = stem_out.shape[0]
    result = jnp.zeros((bands * 56, 64), F32)
    for b in range(4):
        result += mm(taps[b], stem[:, 64 * b : 64 * b + 64])
    stem_out[...] = result.reshape(bands, 7, 8, 64)[:, :, :7, :]


def solution(mesh):
    n_row, n_col, dates = mesh.shape["row"], mesh.shape["col"], mesh.shape["date"]

    def local(pixels, w_stem, w_head, pool_grid, neg_index, key_date):
        _, tiles, bands, height, width = pixels.shape
        fr, fc = height // 2, width // 2
        cells = fr // CELL * (fc // CELL)
        anchors = tiles * cells
        w_taps = jnp.transpose(w_stem, (1, 2, 3, 0))
        grid_t = pool_grid.T
        neg = jnp.transpose(neg_index[0], (1, 2, 0, 3)).reshape(anchors, -1)
        place = np.zeros((fc, LANES), np.float32)
        for j in range(fc):
            for t in range(tiles):
                place[j, t * HALF + j] = 1
        groups, half, n_chip = (bands + 1) // 2, 256 // n_row, n_col * dates
        owners = min(n_chip, half // 16)
        vmem = pl.BlockSpec(memory_space=pltpu.VMEM)
        dma = pltpu.SemaphoreType.DMA
        cols, edge, halo, rows, taps = tables(tiles, bands, height, width)
        operands = (
            pixels[0], edge, w_taps, taps, grid_t, jnp.asarray(place, BF), neg, cols, halo, rows,
            w_head, key_date,
        )
        operands = [pltpu.with_memory_space_constraint(x, pltpu.HBM) for x in operands]
        loss, stem = pl.pallas_call(
            functools.partial(kernel, (tiles, bands, height, width, n_row, n_col, dates)),
            out_shape=(
                jax.ShapeDtypeStruct((fc // CELL, tiles, fr // CELL), F32),
                jax.ShapeDtypeStruct((256, 256), BF),
            ),
            in_specs=[pl.BlockSpec(memory_space=pltpu.HBM)] * len(operands),
            out_specs=(vmem, vmem),
            scratch_shapes=[pltpu.VMEM(x.shape, x.dtype) for x in operands[:-1]]
            + [pltpu.SMEM(key_date.shape, key_date.dtype)]
            + [
                pltpu.VMEM((bands, height, tiles * LANES), BF),
                pltpu.VMEM((2, groups, 16, height), BF),
                pltpu.VMEM((2, groups, 16, height), BF),
                pltpu.VMEM((height // 16, bands, 16, 2 * LANES), BF),
                pltpu.VMEM((height + 6, 2, 16, LANES), BF),
                pltpu.VMEM((256, 256), BF),
                pltpu.VMEM((fr, LANES), F32),
                pltpu.VMEM((neg.shape[1] * anchors // LANES, LANES), F32),
                pltpu.VMEM((anchors, anchors), F32),
                pltpu.VMEM((anchors, anchors), F32),
                pltpu.VMEM((dates, *neg.shape), BF),
                pltpu.VMEM((fr // STEP, anchors, STEP * LANES), BF),
                pltpu.VMEM((fr // STEP, 64, STEP * LANES), BF),
                pltpu.VMEM((dates, anchors // 2 + 8, LANES), BF),
                pltpu.VMEM((64, LANES), F32),
                pltpu.VMEM((256, 256), F32),
                pltpu.VMEM((n_row, half, 256), BF),
                pltpu.VMEM((n_row, half, 256), BF),
                pltpu.VMEM((owners, half // owners, 256), BF),
                pltpu.VMEM((n_chip, half // owners, 256), BF),
                pltpu.VMEM((n_row, owners, half // owners, 256), BF),
                dma((2,)), dma((2,)), dma((2,)), dma((2,)),
                dma((dates,)), dma((dates,)), dma((dates,)), dma((dates,)),
                dma((n_row,)), dma((n_row,)), dma((n_chip,)), dma((n_chip,)), dma((n_chip,)), dma((n_chip,)),
                dma((n_row, owners)), dma((n_row, owners)), dma((len(operands),)),
            ],
            compiler_params=pltpu.CompilerParams(
                collective_id=0, has_side_effects=True, vmem_limit_bytes=32 * 2**20
            ),
        )(*operands)
        loss, stem, head = pl.pallas_call(
            finish,
            out_shape=(
                jax.ShapeDtypeStruct(loss.shape, F32),
                jax.ShapeDtypeStruct((bands, 7, 7, 64), F32),
                jax.ShapeDtypeStruct((64, LANES), F32),
            ),
            in_specs=[vmem] * 3,
            out_specs=(vmem, vmem, vmem),
            compiler_params=pltpu.CompilerParams(vmem_limit_bytes=8 * 2**20),
        )(loss, stem, taps)
        loss = loss.transpose(1, 2, 0)[None]
        return loss, jnp.transpose(stem, (3, 0, 1, 2)), head

    return jax.shard_map(
        local,
        mesh=mesh,
        in_specs=(
            P(("groups", "date"), None, None, "row", "col"),
            P(),
            P(),
            P("row", "col"),
            P(("groups", "date"), None, "row", "col", None),
            P(),
        ),
        out_specs=(
            P(("groups", "date"), None, "row", "col"),
            P("groups", None, None, None),
            P("groups", None),
        ),
        check_vma=False,
    )
```

```python
import functools
import math

import jax
import jax.numpy as jnp
import numpy as np
from jax import lax
from jax.experimental import pallas as pl
from jax.experimental.pallas import tpu as pltpu
from jax.sharding import PartitionSpec as P

CELL = 8
TEMP = 0.2
EPS = 1e-06
STEP = 48
LANES = 128
HALF = 64

MESH = pl.DeviceIdType.MESH
BF = jnp.bfloat16
F32 = jnp.float32


def mm(left, right):
    return lax.dot_general(left, right, (((1,), (0,)), ((), ())), preferred_element_type=F32)


def split(array):
    high = array.astype(BF)
    return high, (array - high.astype(F32)).astype(BF)


def dot_3(left, right, over):
    (a, b), (c, d) = split(left), split(right)

    def one(x, y):
        return lax.dot_general(x, y, (over, ((), ())), preferred_element_type=F32)

    return one(a, c) + (one(a, d) + one(b, c))


def mm_high(left, right):
    return dot_3(left, right, ((1,), (0,)))


def fold(array):
    half = array.shape[0] // 2
    return jnp.concatenate([array[:half], array[half:]], axis=1)


def unfold(array):
    half = array.shape[1] // 2
    return jnp.concatenate([array[:, :half], array[:, half:]], axis=0)


def mm_nt(left, right):
    return lax.dot_general(left, right, (((1,), (1,)), ((), ())), preferred_element_type=F32)


def mm_tn(left, right):
    return lax.dot_general(left, right, (((0,), (0,)), ((), ())), preferred_element_type=F32)


def high_nt(left, right):
    return dot_3(left, right, ((1,), (1,)))


def high_tn(left, right):
    return dot_3(left, right, ((0,), (0,)))


def tables(tiles, bands, height, width):
    cols = np.zeros((tiles * LANES, 2 * LANES), np.float32)
    edge = np.zeros((2, 32, tiles * LANES), np.float32)
    halo = np.zeros((32, 2, 2 * LANES), np.float32)
    for t in range(tiles):
        for w in range(width):
            q = w + 3
            cols[t * LANES + w, (q % 2) * LANES + t * HALF + q // 2] = 1
        for k in range(3):
            for p in range(2):
                spot = p * 8 + t * 3 + k
                edge[p, spot, t * LANES + width - 3 + k] = 1
                edge[p, 16 + spot, t * LANES + k] = 1
                halo[spot, p, (k % 2) * LANES + t * HALF + k // 2] = 1
                q = width + 3 + k
                halo[16 + spot, p, (q % 2) * LANES + t * HALF + q // 2] = 1
    rows = np.zeros((16, 16, bands, 16), np.float32)
    for r in range(16):
        for c in range(bands):
            rows[r, c, c, r] = 1
    taps = np.zeros((4, bands, 7, 8, 8, 2, 16), np.float32)
    for b in range(4):
        for c in range(bands):
            for u in range(7):
                for pc in range(2):
                    if 2 * b + pc < 7:
                        taps[b, c, u, 2 * b + pc, u, pc, c] = 1
    tables = (
        cols, edge, halo.reshape(32, 4 * LANES), rows.reshape(256, bands * 16), taps.reshape(4, bands * 56, 256),
    )
    return [jnp.asarray(x, BF) for x in tables]


def kernel(
    sizes,
    *refs,
):
    n_in = 12
    sources, outs = refs[:n_in], refs[n_in : n_in + 2]
    held, rest = refs[n_in + 2 : 2 * n_in + 2], refs[2 * n_in + 2 :]
    body(sizes, sources, held, *outs, *held, *rest)


def body(
    sizes, sources, held, loss_out, stem_out,
    pix, edge, w_taps, taps, grid_t, place, neg, cols, halo, rows, w_head, key_date,
    both_pix, pack, strips, blocks, image, w_all, gids, neg_t, count_t, count_s, negs, member, hidden,
    keys, g_head, g_acc, part, got_1, part_2, got_2, got_4,
    s_col, r_col, s_row, r_row, s_key, r_key, s_neg, r_neg, s_1, r_1, s_2, r_2, s_3, r_3, s_4, r_4,
    s_in,
):
    tiles, bands, height, width, n_row, n_col, dates = sizes
    fr, fc = height // 2, width // 2
    cells = fr // CELL * (fc // CELL)
    anchors = tiles * cells
    n_mem = n_row * n_col
    row, col, date = lax.axis_index("row"), lax.axis_index("col"), lax.axis_index("date")

    fetches = [pltpu.make_async_copy(a, b, s_in.at[i]) for i, (a, b) in enumerate(zip(sources, held))]
    for c in fetches:
        c.start()
    barrier = pltpu.get_barrier_semaphore()

    def paired(value, mask, count):
        if count & (count - 1):
            return lax.rem(value + mask, count)
        k = 1
        while k < count:
            if mask & k:
                value = value + k - 2 * k * lax.rem(value // k, 2)
            k *= 2
        return value

    def others(name, count, mine):
        found = []
        for k in range(count - 1, 0, -1):
            other = paired(mine, k, count)
            found.append((other, {name: other}))
        return found

    rows_of, peers = others("row", n_row, row), others("date", dates, date)
    n_chip = n_col * dates
    chip = col * dates + date
    chips = []
    steps = [(a, b) for a in range(n_col) for b in range(dates) if a + b > 0]
    for a, b in sorted(steps, key=lambda step: (-sum(step), step)):
        to_col, to_date = paired(col, a, n_col), paired(date, b, dates)
        chips.append((to_col * dates + to_date, {"col": to_col, "date": to_date}))
    for _, dev in rows_of + chips:
        pl.semaphore_signal(barrier, inc=1, device_id=dev, device_id_type=MESH)

    fetches[0].wait()
    fetches[1].wait()

    for c in range(bands):
        flat = []
        for t in range(tiles):
            flat += [pix[t, c], jnp.zeros((height, LANES - width), BF)]
        both_pix[c] = jnp.concatenate(flat, axis=1)
    for g in range((bands + 1) // 2):
        ends = mm_nt(edge[0], both_pix[2 * g]).astype(BF)
        if 2 * g + 1 < bands:
            ends += mm_nt(edge[1], both_pix[2 * g + 1]).astype(BF)
        pack[0, g] = ends[:16]
        pack[1, g] = ends[16:]

    pl.semaphore_wait(barrier, len(rows_of) + len(chips))

    def copy(src, dst, send, recv, dev):
        return pltpu.make_async_remote_copy(
            src_ref=src, dst_ref=dst, send_sem=send, recv_sem=recv,
            device_id=dev, device_id_type=MESH,
        )

    to_right = copy(pack.at[0], strips.at[0], s_col.at[0], r_col.at[0], {"col": lax.rem(col + 1, n_col)})
    to_left = copy(pack.at[1], strips.at[1], s_col.at[1], r_col.at[1], {"col": lax.rem(col + n_col - 1, n_col)})
    down = copy(image.at[pl.ds(height, 3)], image.at[pl.ds(0, 3)], s_row.at[0], r_row.at[0], {"row": lax.rem(row + 1, n_row)})
    up = copy(image.at[pl.ds(3, 3)], image.at[pl.ds(height + 3, 3)], s_row.at[1], r_row.at[1], {"row": lax.rem(row + n_row - 1, n_row)})

    @pl.when(col < n_col - 1)
    def _():
        to_right.start()

    @pl.when(col > 0)
    def _():
        to_left.start()

    @pl.when(col == 0)
    def _():
        strips[0] = jnp.zeros(strips.shape[1:], BF)

    @pl.when(col == n_col - 1)
    def _():
        strips[1] = jnp.zeros(strips.shape[1:], BF)

    for c in fetches[2:]:
        c.wait()
    negs[pl.ds(date, 1)] = neg[...].astype(F32).astype(BF)[None]
    sends = [copy(negs.at[date], negs.at[date], s_neg.at[o], r_neg.at[date], dev) for o, dev in peers]
    for c in sends:
        c.start()

    for c in range(bands):
        wide = mm(both_pix[c], cols[...]).astype(BF)
        blocks[:, c] = wide.reshape(height // 16, 16, 2 * LANES)

    w_flat = w_taps[...].astype(F32)
    w_flat = jnp.concatenate([w_flat, jnp.zeros((bands, 7, 1, 64), F32)], axis=2)
    w_flat = w_flat.reshape(bands * 56, 64).astype(BF)
    for b in range(4):
        w_all[64 * b : 64 * b + 64, :] = mm_tn(w_flat, taps[b]).astype(BF)
    lane = lax.broadcasted_iota(jnp.int32, (1, LANES), 1)
    inside = lax.rem(lane, HALF) < fc
    shift = jnp.where(inside, (lane // HALF) * cells, -1000).astype(F32)
    gids[...] = mm_tn(grid_t[...].astype(F32).astype(BF), place[...]) + shift
    sub = lax.broadcasted_iota(jnp.int32, (anchors, 1), 0)
    key_ids = (lax.rem(sub, tiles) * cells + sub // tiles).astype(F32)
    n_neg = neg.shape[1]
    rest = anchors - LANES
    split = LANES // rest
    per = n_neg // split

    def at(axis, shape):
        return lax.broadcasted_iota(jnp.int32, shape, axis)

    def ones_at(mask):
        return mask.astype(F32).astype(BF)

    square = (n_neg, n_neg)
    eye_n = ones_at(at(0, square) == at(1, square))
    fold_n = ones_at(at(0, (per, n_neg)) == lax.rem(at(1, (per, n_neg)), per))
    in_group = at(0, (LANES, n_neg)) // rest == at(1, (LANES, n_neg)) // per
    regroup = ones_at(lax.rem(at(0, (LANES, rest)), rest) == at(1, (LANES, rest)))

    def count_keys(index):
        neg_t[:n_neg] = mm_nt(eye_n, index[:LANES])
        tail = jnp.where(in_group, jnp.concatenate([index[LANES:].astype(F32)] * split, axis=0), 0.0)
        neg_t[n_neg:] = mm_nt(fold_n, tail.astype(BF))

        def count_step(s, total):
            for k in range(8):
                total += jnp.where(neg_t[pl.ds(s * 8 + k, 1), :] == key_ids, 1.0, 0.0)
            return total

        first = lax.fori_loop(0, n_neg // 8, count_step, jnp.zeros((anchors, LANES), F32))
        last = lax.fori_loop(n_neg // 8, (n_neg + per) // 8, count_step, jnp.zeros((anchors, LANES), F32))
        return jnp.concatenate([first, mm(last.astype(BF), regroup)], axis=1)

    def member_step(i, carry):
        for k in range(8):
            r = i * 8 + k
            member[r] = jnp.where(gids[pl.ds(r, 1), :] == key_ids, 1.0, 0.0).astype(BF)
        return carry

    lax.fori_loop(0, fr // 8, member_step, 0)

    def members_of(s):
        return jnp.concatenate([member[s * STEP + r] for r in range(STEP)], axis=1)

    @pl.when(col > 0)
    def _():
        copy(pack.at[0], strips.at[0], s_col.at[0], r_col.at[0], {"col": lax.rem(col + n_col - 1, n_col)}).wait_recv()

    @pl.when(col < n_col - 1)
    def _():
        copy(pack.at[1], strips.at[1], s_col.at[1], r_col.at[1], {"col": lax.rem(col + 1, n_col)}).wait_recv()

    for g in range((bands + 1) // 2):
        ends = mm_tn(jnp.concatenate([strips[0, g], strips[1, g]], axis=0), halo[...]).astype(BF)
        for p in range(min(2, bands - 2 * g)):
            wide = ends[:, 2 * LANES * p : 2 * LANES * (p + 1)].reshape(height // 16, 16, 2 * LANES)
            blocks[:, 2 * g + p] += wide

    def image_step(k):
        out = mm(rows[...], blocks[k].reshape(bands * 16, 2 * LANES)).astype(BF)
        for pc in range(2):
            image[pl.ds(16 * k + 3, 16), pc] = out[:, pc * LANES : (pc + 1) * LANES].reshape(16, 16, LANES)

    image_step(height // 16 - 1)
    image_step(0)

    @pl.when(row < n_row - 1)
    def _():
        down.start()

    @pl.when(row > 0)
    def _():
        up.start()

    @pl.when(row == 0)
    def _():
        image[:3] = jnp.zeros((3, *image.shape[1:]), BF)

    @pl.when(row == n_row - 1)
    def _():
        image[height + 3 :] = jnp.zeros((3, *image.shape[1:]), BF)

    for k in range(1, height // 16 - 1):
        image_step(k)

    @pl.when(row > 0)
    def _():
        copy(image.at[pl.ds(height, 3)], image.at[pl.ds(0, 3)], s_row.at[0], r_row.at[0], {"row": lax.rem(row + n_row - 1, n_row)}).wait_recv()

    @pl.when(row < n_row - 1)
    def _():
        copy(image.at[pl.ds(3, 3)], image.at[pl.ds(height + 3, 3)], s_row.at[1], r_row.at[1], {"row": lax.rem(row + 1, n_row)}).wait_recv()

    def wide_rows(s):
        return jnp.concatenate(
            [image[pl.ds(2 * (s * STEP + r), 8)].reshape(256, LANES) for r in range(STEP)], axis=1
        )

    def forward_step(s, total):
        taps_out = mm(w_all[...], wide_rows(s))
        hid = []
        for r in range(STEP):
            part_r = taps_out[:, r * LANES : (r + 1) * LANES]
            stem = part_r[:64]
            for b in range(1, 4):
                stem += pltpu.roll(part_r[64 * b : 64 * b + 64], LANES - b, 1)
            hid.append(jnp.maximum(stem, 0.0).astype(BF))
        hid = jnp.concatenate(hid, axis=1)
        hidden[s] = hid
        return total + mm_nt(members_of(s), jnp.concatenate([hid, jnp.ones_like(hid)], axis=0))

    sums = lax.fori_loop(0, fr // STEP, forward_step, jnp.zeros((anchors, LANES), F32))
    counts = sums[:, 64:]
    pooled = sums[:, :64] / counts
    head = w_head[...]
    project = mm_high(pooled, head)
    length = jnp.sqrt(jnp.sum(project * project, axis=1, keepdims=True) + EPS)
    embed = project / length
    short = pooled / length
    folded = fold(short)
    mean = jnp.mean(folded, axis=0, keepdims=True)
    away = folded - mean
    base = [away]
    for _ in range(3):
        term = mean.astype(BF).astype(F32)
        base.append(term)
        mean = mean - term
    base.append(jnp.zeros((5, LANES), F32))
    keys[pl.ds(date, 1)] = jnp.concatenate(base, axis=0).astype(BF)[None]
    key_sends = [copy(keys.at[date], keys.at[date], s_key.at[o], r_key.at[date], dev) for o, dev in peers]
    for c in key_sends:
        c.start()
    back = high_nt(embed, head)
    for o, dev in peers:
        copy(negs.at[o], negs.at[o], s_neg.at[o], r_neg.at[o], dev).wait_recv()
    target = key_date[date]
    source = 0
    for d in range(dates):
        source = jnp.where(key_date[d] == date, d, source)
    count_t[...] = count_keys(negs[date])
    count_s[...] = count_keys(negs[source])
    for o, dev in peers:
        copy(keys.at[o], keys.at[o], s_key.at[o], r_key.at[o], dev).wait_recv()
    key_rows = anchors // 2

    def received(d):
        whole = keys[d].astype(F32)
        mean = whole[key_rows : key_rows + 1] + whole[key_rows + 1 : key_rows + 2] + whole[key_rows + 2 : key_rows + 3]
        return unfold(whole[:key_rows] + mean)

    key_short, own_short = received(target), received(source)
    same = lax.broadcasted_iota(jnp.int32, (anchors, anchors), 0) == lax.broadcasted_iota(
        jnp.int32, (anchors, anchors), 1
    )
    scale = 1.0 / math.sqrt(dates * anchors * n_mem)

    def contrast(scores, count):
        positive = jnp.sum(jnp.where(same, scores, 0.0), axis=0, keepdims=True)
        weights = count * jnp.exp(scores)
        exp_pos = jnp.exp(positive)
        denominator = exp_pos + jnp.sum(weights, axis=0, keepdims=True)
        d_scores = (scale / TEMP) * (
            weights / denominator + jnp.where(same, exp_pos / denominator - 1.0, 0.0)
        )
        return d_scores, jnp.log(denominator) - positive

    d_scores, losses = contrast(high_nt(key_short, back) / TEMP, count_t[...])
    d_source, _ = contrast(high_nt(back, own_short) / TEMP, count_s[...])
    grad_short = high_tn(d_scores, key_short) + mm_high(d_source, own_short)
    n_down, n_across = fr // CELL, fc // CELL
    wide = n_across * tiles
    spot = lax.broadcasted_iota(jnp.int32, (wide, anchors), 1)
    pick = jnp.where(lax.rem(spot, wide) == lax.broadcasted_iota(jnp.int32, (wide, anchors), 0), losses, 0.0)
    line = lax.broadcasted_iota(jnp.int32, (n_down, anchors), 1) // wide
    lines = (line == lax.broadcasted_iota(jnp.int32, (n_down, anchors), 0)).astype(F32)
    loss_out[...] = high_nt(pick, lines).reshape(n_across, tiles, n_down)
    grad_embed = mm_high(grad_short, head)
    grad_project = (
        grad_embed - embed * jnp.sum(embed * grad_embed, axis=1, keepdims=True)
    ) / length
    head_term = high_tn(pooled, grad_project)
    sends += key_sends
    g_head[...] = head_term
    per_cell = (high_nt(grad_project, head) / counts).astype(BF)
    eye_c = (
        lax.broadcasted_iota(jnp.int32, (64, 64), 0) == lax.broadcasted_iota(jnp.int32, (64, 64), 1)
    ).astype(F32).astype(BF)
    cell_t = mm_nt(eye_c, per_cell).astype(BF)

    g_acc[...] = jnp.zeros_like(g_acc)

    def backward_step(s, carry):
        spread = mm(cell_t, members_of(s))
        slope = jnp.where(hidden[s] > 0, spread.astype(BF), jnp.zeros((), BF))
        moved = [slope]
        for b in range(1, 4):
            moved.append(
                jnp.concatenate(
                    [pltpu.roll(slope[:, r * LANES : (r + 1) * LANES], b, 1) for r in range(STEP)], axis=1
                )
            )
        g_acc[...] += mm_nt(wide_rows(s), jnp.concatenate(moved, axis=0))
        return carry

    lax.fori_loop(0, fr // STEP, backward_step, 0)

    g_acc[224:, :LANES] = g_head[:32]
    g_acc[224:, LANES:] = g_head[32:]
    gr = 256 // n_row
    owners = min(n_chip, gr // 16)
    every = owners == n_chip
    part[...] = g_acc[...].astype(BF).reshape(n_row, gr, 256)
    step_1 = [copy(part.at[o], got_1.at[row], s_1.at[o], r_1.at[row], dev) for o, dev in rows_of]
    for c in step_1:
        c.start()

    def when(chosen, run):
        if every:
            run()
        else:
            pl.when(chosen)(run)

    total = g_acc[pl.ds(row * gr, gr)]
    for o, dev in rows_of:
        copy(part.at[o], got_1.at[o], s_1.at[o], r_1.at[o], dev).wait_recv()
        total += got_1[pl.ds(o, 1)].reshape(gr, 256).astype(F32)
    part_2[...] = total.astype(BF).reshape(part_2.shape)
    step_2 = [copy(part_2.at[o], got_2.at[chip], s_2.at[o], r_2.at[chip], dev) for o, dev in chips]
    for (o, _), c in zip(chips, step_2):
        when(o < owners, c.start)
    across = [copy(got_4.at[row, chip], got_4.at[row, chip], s_3.at[o], r_3.at[chip], dev) for o, dev in chips]

    def own_chunk():
        got_2[pl.ds(chip, 1)] = part_2[pl.ds(chip, 1)]
        for o, dev in chips:
            copy(got_2.at[o], got_2.at[o], s_2.at[o], r_2.at[o], dev).wait_recv()
        total = got_2[0].astype(F32)
        for m in range(1, n_chip):
            total += got_2[m].astype(F32)
        got_4[row, pl.ds(chip, 1)] = total.astype(BF)[None]
        for c in across:
            c.start()

    when(chip < owners, own_chunk)

    def pass_on(o):
        return [copy(got_4.at[row, o], got_4.at[row, o], s_4.at[k, o], r_4.at[row, o], dev) for k, dev in rows_of]

    def start_all(copies):
        for c in copies:
            c.start()

    when(chip < owners, lambda: start_all(pass_on(chip)))
    for o, dev in chips:
        def arrived(o=o, dev=dev):
            copy(got_4.at[row, o], got_4.at[row, o], s_3.at[o], r_3.at[o], dev).wait_recv()
            start_all(pass_on(o))

        when(o < owners, arrived)
    for k, dev in rows_of:
        for o in range(owners):
            copy(got_4.at[k, o], got_4.at[k, o], s_4.at[k, o], r_4.at[k, o], dev).wait_recv()
    stem_out[...] = got_4[...].reshape(256, 256)

    for (o, _), c in zip(chips, step_2):
        when(o < owners, c.wait_send)
    when(chip < owners, lambda: [c.wait_send() for c in across] and None)
    for o in range(owners):
        for c in pass_on(o):
            c.wait_send()
    sends += step_1
    for c in sends:
        c.wait_send()

    @pl.when(col < n_col - 1)
    def _():
        to_right.wait_send()

    @pl.when(col > 0)
    def _():
        to_left.wait_send()

    @pl.when(row < n_row - 1)
    def _():
        down.wait_send()

    @pl.when(row > 0)
    def _():
        up.wait_send()


def finish(loss, stem, taps, loss_out, stem_out, head_out):
    loss_out[...] = loss[...]
    head_out[...] = unfold(stem[224:].astype(F32))
    bands = stem_out.shape[0]
    result = jnp.zeros((bands * 56, 64), F32)
    for b in range(4):
        result += mm(taps[b], stem[:, 64 * b : 64 * b + 64])
    stem_out[...] = result.reshape(bands, 7, 8, 64)[:, :, :7, :]


def solution(mesh):
    n_row, n_col, dates = mesh.shape["row"], mesh.shape["col"], mesh.shape["date"]

    def local(pixels, w_stem, w_head, pool_grid, neg_index, key_date):
        _, tiles, bands, height, width = pixels.shape
        fr, fc = height // 2, width // 2
        cells = fr // CELL * (fc // CELL)
        anchors = tiles * cells
        w_taps = jnp.transpose(w_stem, (1, 2, 3, 0))
        grid_t = pool_grid.T
        neg = jnp.transpose(neg_index[0], (1, 2, 0, 3)).reshape(anchors, -1)
        place = np.zeros((fc, LANES), np.float32)
        for j in range(fc):
            for t in range(tiles):
                place[j, t * HALF + j] = 1
        groups, half, n_chip = (bands + 1) // 2, 256 // n_row, n_col * dates
        owners = min(n_chip, half // 16)
        vmem = pl.BlockSpec(memory_space=pltpu.VMEM)
        dma = pltpu.SemaphoreType.DMA
        cols, edge, halo, rows, taps = tables(tiles, bands, height, width)
        operands = (
            pixels[0], edge, w_taps, taps, grid_t, jnp.asarray(place, BF), neg, cols, halo, rows,
            w_head, key_date,
        )
        operands = [pltpu.with_memory_space_constraint(x, pltpu.HBM) for x in operands]
        loss, stem = pl.pallas_call(
            functools.partial(kernel, (tiles, bands, height, width, n_row, n_col, dates)),
            out_shape=(
                jax.ShapeDtypeStruct((fc // CELL, tiles, fr // CELL), F32),
                jax.ShapeDtypeStruct((256, 256), BF),
            ),
            in_specs=[pl.BlockSpec(memory_space=pltpu.HBM)] * len(operands),
            out_specs=(vmem, vmem),
            scratch_shapes=[pltpu.VMEM(x.shape, x.dtype) for x in operands[:-1]]
            + [pltpu.SMEM(key_date.shape, key_date.dtype)]
            + [
                pltpu.VMEM((bands, height, tiles * LANES), BF),
                pltpu.VMEM((2, groups, 16, height), BF),
                pltpu.VMEM((2, groups, 16, height), BF),
                pltpu.VMEM((height // 16, bands, 16, 2 * LANES), BF),
                pltpu.VMEM((height + 6, 2, 16, LANES), BF),
                pltpu.VMEM((256, 256), BF),
                pltpu.VMEM((fr, LANES), F32),
                pltpu.VMEM((neg.shape[1] * anchors // LANES, LANES), F32),
                pltpu.VMEM((anchors, anchors), F32),
                pltpu.VMEM((anchors, anchors), F32),
                pltpu.VMEM((dates, *neg.shape), BF),
                pltpu.VMEM((fr, anchors, LANES), BF),
                pltpu.VMEM((fr // STEP, 64, STEP * LANES), BF),
                pltpu.VMEM((dates, anchors // 2 + 8, LANES), BF),
                pltpu.VMEM((64, LANES), F32),
                pltpu.VMEM((256, 256), F32),
                pltpu.VMEM((n_row, half, 256), BF),
                pltpu.VMEM((n_row, half, 256), BF),
                pltpu.VMEM((owners, half // owners, 256), BF),
                pltpu.VMEM((n_chip, half // owners, 256), BF),
                pltpu.VMEM((n_row, owners, half // owners, 256), BF),
                dma((2,)), dma((2,)), dma((2,)), dma((2,)),
                dma((dates,)), dma((dates,)), dma((dates,)), dma((dates,)),
                dma((n_row,)), dma((n_row,)), dma((n_chip,)), dma((n_chip,)), dma((n_chip,)), dma((n_chip,)),
                dma((n_row, owners)), dma((n_row, owners)), dma((len(operands),)),
            ],
            compiler_params=pltpu.CompilerParams(
                collective_id=0, has_side_effects=True, vmem_limit_bytes=32 * 2**20
            ),
        )(*operands)
        loss, stem, head = pl.pallas_call(
            finish,
            out_shape=(
                jax.ShapeDtypeStruct(loss.shape, F32),
                jax.ShapeDtypeStruct((bands, 7, 7, 64), F32),
                jax.ShapeDtypeStruct((64, LANES), F32),
            ),
            in_specs=[vmem] * 3,
            out_specs=(vmem, vmem, vmem),
            compiler_params=pltpu.CompilerParams(vmem_limit_bytes=8 * 2**20),
        )(loss, stem, taps)
        loss = loss.transpose(1, 2, 0)[None]
        return loss, jnp.transpose(stem, (3, 0, 1, 2)), head

    return jax.shard_map(
        local,
        mesh=mesh,
        in_specs=(
            P(("groups", "date"), None, None, "row", "col"),
            P(),
            P(),
            P("row", "col"),
            P(("groups", "date"), None, "row", "col", None),
            P(),
        ),
        out_specs=(
            P(("groups", "date"), None, "row", "col"),
            P("groups", None, None, None),
            P("groups", None),
        ),
        check_vma=False,
    )
```

```python
import functools
import math

import jax
import jax.numpy as jnp
import numpy as np
from jax import lax
from jax.experimental import pallas as pl
from jax.experimental.pallas import tpu as pltpu
from jax.sharding import PartitionSpec as P

CELL = 8
TEMP = 0.2
EPS = 1e-06
STEP = 48
LANES = 128
HALF = 64

MESH = pl.DeviceIdType.MESH
BF = jnp.bfloat16
F32 = jnp.float32


def mm(left, right):
    return lax.dot_general(left, right, (((1,), (0,)), ((), ())), preferred_element_type=F32)


def split(array):
    high = array.astype(BF)
    return high, (array - high.astype(F32)).astype(BF)


def dot_3(left, right, over):
    (a, b), (c, d) = split(left), split(right)

    def one(x, y):
        return lax.dot_general(x, y, (over, ((), ())), preferred_element_type=F32)

    return one(a, c) + (one(a, d) + one(b, c))


def mm_high(left, right):
    return dot_3(left, right, ((1,), (0,)))


def fold(array):
    half = array.shape[0] // 2
    return jnp.concatenate([array[:half], array[half:]], axis=1)


def unfold(array):
    half = array.shape[1] // 2
    return jnp.concatenate([array[:, :half], array[:, half:]], axis=0)


def mm_nt(left, right):
    return lax.dot_general(left, right, (((1,), (1,)), ((), ())), preferred_element_type=F32)


def mm_tn(left, right):
    return lax.dot_general(left, right, (((0,), (0,)), ((), ())), preferred_element_type=F32)


def high_nt(left, right):
    return dot_3(left, right, ((1,), (1,)))


def high_tn(left, right):
    return dot_3(left, right, ((0,), (0,)))


def tables(tiles, bands, height, width):
    cols = np.zeros((tiles * LANES, 2 * LANES), np.float32)
    edge = np.zeros((2, 32, tiles * LANES), np.float32)
    halo = np.zeros((32, 2, 2 * LANES), np.float32)
    for t in range(tiles):
        for w in range(width):
            q = w + 3
            cols[t * LANES + w, (q % 2) * LANES + t * HALF + q // 2] = 1
        for k in range(3):
            for p in range(2):
                spot = p * 8 + t * 3 + k
                edge[p, spot, t * LANES + width - 3 + k] = 1
                edge[p, 16 + spot, t * LANES + k] = 1
                halo[spot, p, (k % 2) * LANES + t * HALF + k // 2] = 1
                q = width + 3 + k
                halo[16 + spot, p, (q % 2) * LANES + t * HALF + q // 2] = 1
    rows = np.zeros((16, 16, bands, 16), np.float32)
    for r in range(16):
        for c in range(bands):
            rows[r, c, c, r] = 1
    taps = np.zeros((4, bands, 7, 8, 8, 2, 16), np.float32)
    for b in range(4):
        for c in range(bands):
            for u in range(7):
                for pc in range(2):
                    if 2 * b + pc < 7:
                        taps[b, c, u, 2 * b + pc, u, pc, c] = 1
    tables = (
        cols, edge, halo.reshape(32, 4 * LANES), rows.reshape(256, bands * 16), taps.reshape(4, bands * 56, 256),
    )
    return [jnp.asarray(x, BF) for x in tables]


def kernel(
    sizes,
    *refs,
):
    n_in = 12
    sources, outs, taps = refs[:n_in], refs[n_in : n_in + 2], refs[n_in + 2]
    held, rest = refs[n_in + 3 : 2 * n_in + 2], refs[2 * n_in + 2 :]
    held = (*held[:3], taps, *held[3:])
    body(sizes, sources, held, *outs, *held, *rest)


def body(
    sizes, sources, held, loss_out, stem_out,
    pix, edge, w_taps, taps, grid_t, place, neg, cols, halo, rows, w_head, key_date,
    both_pix, pack, strips, blocks, image, w_all, gids, neg_t, count_t, count_s, negs, member, hidden,
    cell_count, keys, g_head, g_acc, part, got_1, part_2, got_2, got_4,
    s_col, r_col, s_row, r_row, s_key, r_key, s_neg, r_neg, s_1, r_1, s_2, r_2, s_3, r_3, s_4, r_4,
    s_in,
):
    tiles, bands, height, width, n_row, n_col, dates = sizes
    fr, fc = height // 2, width // 2
    cells = fr // CELL * (fc // CELL)
    anchors = tiles * cells
    n_mem = n_row * n_col
    row, col, date = lax.axis_index("row"), lax.axis_index("col"), lax.axis_index("date")

    fetches = [pltpu.make_async_copy(a, b, s_in.at[i]) for i, (a, b) in enumerate(zip(sources, held))]
    for c in fetches[:2]:
        c.start()
    barrier = pltpu.get_barrier_semaphore()

    def paired(value, mask, count):
        if count & (count - 1):
            return lax.rem(value + mask, count)
        k = 1
        while k < count:
            if mask & k:
                value = value + k - 2 * k * lax.rem(value // k, 2)
            k *= 2
        return value

    def others(name, count, mine):
        found = []
        for k in range(count - 1, 0, -1):
            other = paired(mine, k, count)
            found.append((other, {name: other}))
        return found

    rows_of, peers = others("row", n_row, row), others("date", dates, date)
    n_chip = n_col * dates
    chip = col * dates + date
    chips = []
    steps = [(a, b) for a in range(n_col) for b in range(dates) if a + b > 0]
    for a, b in sorted(steps, key=lambda step: (-sum(step), step)):
        to_col, to_date = paired(col, a, n_col), paired(date, b, dates)
        chips.append((to_col * dates + to_date, {"col": to_col, "date": to_date}))
    cols_of = others("col", n_col, col)
    for _, dev in rows_of + cols_of + peers:
        pl.semaphore_signal(barrier, inc=1, device_id=dev, device_id_type=MESH)

    fetches[0].wait()
    fetches[1].wait()
    for c in fetches[2:]:
        c.start()

    for c in range(bands):
        flat = []
        for t in range(tiles):
            flat += [pix[t, c], jnp.zeros((height, LANES - width), BF)]
        both_pix[c] = jnp.concatenate(flat, axis=1)
    for g in range((bands + 1) // 2):
        ends = mm_nt(edge[0], both_pix[2 * g]).astype(BF)
        if 2 * g + 1 < bands:
            ends += mm_nt(edge[1], both_pix[2 * g + 1]).astype(BF)
        pack[0, g] = ends[:16]
        pack[1, g] = ends[16:]

    pl.semaphore_wait(barrier, len(rows_of) + len(cols_of) + len(peers))

    def copy(src, dst, send, recv, dev):
        return pltpu.make_async_remote_copy(
            src_ref=src, dst_ref=dst, send_sem=send, recv_sem=recv,
            device_id=dev, device_id_type=MESH,
        )

    to_right = copy(pack.at[0], strips.at[0], s_col.at[0], r_col.at[0], {"col": lax.rem(col + 1, n_col)})
    to_left = copy(pack.at[1], strips.at[1], s_col.at[1], r_col.at[1], {"col": lax.rem(col + n_col - 1, n_col)})
    down = copy(image.at[pl.ds(height, 3)], image.at[pl.ds(0, 3)], s_row.at[0], r_row.at[0], {"row": lax.rem(row + 1, n_row)})
    up = copy(image.at[pl.ds(3, 3)], image.at[pl.ds(height + 3, 3)], s_row.at[1], r_row.at[1], {"row": lax.rem(row + n_row - 1, n_row)})

    @pl.when(col < n_col - 1)
    def _():
        to_right.start()

    @pl.when(col > 0)
    def _():
        to_left.start()

    @pl.when(col == 0)
    def _():
        strips[0] = jnp.zeros(strips.shape[1:], BF)

    @pl.when(col == n_col - 1)
    def _():
        strips[1] = jnp.zeros(strips.shape[1:], BF)

    for c in fetches[2:]:
        c.wait()

    for c in range(bands):
        wide = mm(both_pix[c], cols[...]).astype(BF)
        blocks[:, c] = wide.reshape(height // 16, 16, 2 * LANES)

    w_flat = w_taps[...].astype(F32)
    w_flat = jnp.concatenate([w_flat, jnp.zeros((bands, 7, 1, 64), F32)], axis=2)
    w_flat = w_flat.reshape(bands * 56, 64).astype(BF)
    for b in range(4):
        w_all[64 * b : 64 * b + 64, :] = mm_tn(w_flat, taps[b]).astype(BF)
    lane = lax.broadcasted_iota(jnp.int32, (1, LANES), 1)
    inside = lax.rem(lane, HALF) < fc
    shift = jnp.where(inside, (lane // HALF) * cells, -1000).astype(F32)
    gids[...] = mm_tn(grid_t[...].astype(F32).astype(BF), place[...]) + shift
    sub = lax.broadcasted_iota(jnp.int32, (anchors, 1), 0)
    key_ids = (lax.rem(sub, tiles) * cells + sub // tiles).astype(F32)
    n_neg = neg.shape[1]
    rest = anchors - LANES
    split = LANES // rest
    per = n_neg // split

    def at(axis, shape):
        return lax.broadcasted_iota(jnp.int32, shape, axis)

    def ones_at(mask):
        return mask.astype(F32).astype(BF)

    square = (n_neg, n_neg)
    eye_n = ones_at(at(0, square) == at(1, square))
    fold_n = ones_at(at(0, (per, n_neg)) == lax.rem(at(1, (per, n_neg)), per))
    in_group = at(0, (LANES, n_neg)) // rest == at(1, (LANES, n_neg)) // per
    regroup = ones_at(lax.rem(at(0, (LANES, rest)), rest) == at(1, (LANES, rest)))

    def count_keys(index):
        neg_t[:n_neg] = mm_nt(eye_n, index[:LANES])
        tail = jnp.where(in_group, jnp.concatenate([index[LANES:].astype(F32)] * split, axis=0), 0.0)
        neg_t[n_neg:] = mm_nt(fold_n, tail.astype(BF))

        def count_step(s, total):
            for k in range(8):
                total += jnp.where(neg_t[pl.ds(s * 8 + k, 1), :] == key_ids, 1.0, 0.0)
            return total

        first = lax.fori_loop(0, n_neg // 8, count_step, jnp.zeros((anchors, LANES), F32))
        last = lax.fori_loop(n_neg // 8, (n_neg + per) // 8, count_step, jnp.zeros((anchors, LANES), F32))
        return jnp.concatenate([first, mm(last.astype(BF), regroup)], axis=1)

    def member_step(i, carry):
        for k in range(8):
            r = i * 8 + k
            here = jnp.where(gids[pl.ds(r, 1), :] == key_ids, 1.0, 0.0)
            member[r] = here.astype(BF)
            carry += here
        return carry

    found = lax.fori_loop(0, fr // 8, member_step, jnp.zeros((anchors, LANES), F32))
    cell_count[...] = jnp.broadcast_to(jnp.sum(found, axis=1, keepdims=True), (anchors, 64))

    def members_of(s):
        return jnp.concatenate([member[s * STEP + r] for r in range(STEP)], axis=1)

    @pl.when(col > 0)
    def _():
        copy(pack.at[0], strips.at[0], s_col.at[0], r_col.at[0], {"col": lax.rem(col + n_col - 1, n_col)}).wait_recv()

    @pl.when(col < n_col - 1)
    def _():
        copy(pack.at[1], strips.at[1], s_col.at[1], r_col.at[1], {"col": lax.rem(col + 1, n_col)}).wait_recv()

    negs[pl.ds(date, 1)] = neg[...].astype(F32).astype(BF)[None]
    sends = [copy(negs.at[date], negs.at[date], s_neg.at[o], r_neg.at[date], dev) for o, dev in peers]
    for c in sends:
        c.start()

    for g in range((bands + 1) // 2):
        ends = mm_tn(jnp.concatenate([strips[0, g], strips[1, g]], axis=0), halo[...]).astype(BF)
        for p in range(min(2, bands - 2 * g)):
            wide = ends[:, 2 * LANES * p : 2 * LANES * (p + 1)].reshape(height // 16, 16, 2 * LANES)
            blocks[:, 2 * g + p] += wide

    def image_step(k):
        out = mm(rows[...], blocks[k].reshape(bands * 16, 2 * LANES)).astype(BF)
        for pc in range(2):
            image[pl.ds(16 * k + 3, 16), pc] = out[:, pc * LANES : (pc + 1) * LANES].reshape(16, 16, LANES)

    image_step(height // 16 - 1)
    image_step(0)

    @pl.when(row < n_row - 1)
    def _():
        down.start()

    @pl.when(row > 0)
    def _():
        up.start()

    @pl.when(row == 0)
    def _():
        image[:3] = jnp.zeros((3, *image.shape[1:]), BF)

    @pl.when(row == n_row - 1)
    def _():
        image[height + 3 :] = jnp.zeros((3, *image.shape[1:]), BF)

    def image_pair(i, carry):
        image_step(2 * i + 1)
        image_step(2 * i + 2)
        return carry

    lax.fori_loop(0, height // 32 - 1, image_pair, 0)

    @pl.when(row > 0)
    def _():
        copy(image.at[pl.ds(height, 3)], image.at[pl.ds(0, 3)], s_row.at[0], r_row.at[0], {"row": lax.rem(row + n_row - 1, n_row)}).wait_recv()

    @pl.when(row < n_row - 1)
    def _():
        copy(image.at[pl.ds(3, 3)], image.at[pl.ds(height + 3, 3)], s_row.at[1], r_row.at[1], {"row": lax.rem(row + 1, n_row)}).wait_recv()

    def wide_rows(s):
        return jnp.concatenate(
            [image[pl.ds(2 * (s * STEP + r), 8)].reshape(256, LANES) for r in range(STEP)], axis=1
        )

    def forward_step(s, total):
        taps_out = mm(w_all[...], wide_rows(s))
        hid = []
        for r in range(STEP):
            part_r = taps_out[:, r * LANES : (r + 1) * LANES]
            stem = part_r[:64]
            for b in range(1, 4):
                stem += pltpu.roll(part_r[64 * b : 64 * b + 64], LANES - b, 1)
            hid.append(jnp.maximum(stem, 0.0).astype(BF))
        hid = jnp.concatenate(hid, axis=1)
        hidden[s] = hid
        return total + mm_nt(members_of(s), hid)

    sums = lax.fori_loop(0, fr // STEP, forward_step, jnp.zeros((anchors, 64), F32))
    counts = cell_count[...]
    pooled = sums / counts
    head = w_head[...]
    project = mm_high(pooled, head)
    length = jnp.sqrt(jnp.sum(project * project, axis=1, keepdims=True) + EPS)
    embed = project / length
    short = pooled / length
    folded = fold(short)
    mean = jnp.mean(folded, axis=0, keepdims=True)
    away = folded - mean
    base = [away]
    for _ in range(3):
        term = mean.astype(BF).astype(F32)
        base.append(term)
        mean = mean - term
    base.append(jnp.zeros((5, LANES), F32))
    keys[pl.ds(date, 1)] = jnp.concatenate(base, axis=0).astype(BF)[None]
    key_sends = [copy(keys.at[date], keys.at[date], s_key.at[o], r_key.at[date], dev) for o, dev in peers]
    for c in key_sends:
        c.start()
    back = high_nt(embed, head)
    for o, dev in peers:
        copy(negs.at[o], negs.at[o], s_neg.at[o], r_neg.at[o], dev).wait_recv()
    target = key_date[date]
    source = 0
    for d in range(dates):
        source = jnp.where(key_date[d] == date, d, source)
    count_t[...] = count_keys(negs[date])
    count_s[...] = count_keys(negs[source])
    for o, dev in peers:
        copy(keys.at[o], keys.at[o], s_key.at[o], r_key.at[o], dev).wait_recv()
    key_rows = anchors // 2

    def received(d):
        whole = keys[d].astype(F32)
        mean = whole[key_rows : key_rows + 1] + whole[key_rows + 1 : key_rows + 2] + whole[key_rows + 2 : key_rows + 3]
        return unfold(whole[:key_rows] + mean)

    key_short, own_short = received(target), received(source)
    same = lax.broadcasted_iota(jnp.int32, (anchors, anchors), 0) == lax.broadcasted_iota(
        jnp.int32, (anchors, anchors), 1
    )
    scale = 1.0 / math.sqrt(dates * anchors * n_mem)

    def contrast(scores, count):
        positive = jnp.sum(jnp.where(same, scores, 0.0), axis=0, keepdims=True)
        weights = count * jnp.exp(scores)
        exp_pos = jnp.exp(positive)
        denominator = exp_pos + jnp.sum(weights, axis=0, keepdims=True)
        d_scores = (scale / TEMP) * (
            weights / denominator + jnp.where(same, exp_pos / denominator - 1.0, 0.0)
        )
        return d_scores, jnp.log(denominator) - positive

    d_scores, losses = contrast(high_nt(key_short, back) / TEMP, count_t[...])
    d_source, _ = contrast(high_nt(back, own_short) / TEMP, count_s[...])
    grad_short = high_tn(d_scores, key_short) + mm_high(d_source, own_short)
    n_down, n_across = fr // CELL, fc // CELL
    wide = n_across * tiles
    spot = lax.broadcasted_iota(jnp.int32, (wide, anchors), 1)
    pick = jnp.where(lax.rem(spot, wide) == lax.broadcasted_iota(jnp.int32, (wide, anchors), 0), losses, 0.0)
    line = lax.broadcasted_iota(jnp.int32, (n_down, anchors), 1) // wide
    lines = (line == lax.broadcasted_iota(jnp.int32, (n_down, anchors), 0)).astype(F32)
    loss_out[...] = high_nt(pick, lines).reshape(n_across, tiles, n_down)
    grad_embed = mm_high(grad_short, head)
    grad_project = (
        grad_embed - embed * jnp.sum(embed * grad_embed, axis=1, keepdims=True)
    ) / length
    head_term = high_tn(pooled, grad_project)
    sends += key_sends
    g_head[...] = head_term
    per_cell = (high_nt(grad_project, head) / counts).astype(BF)
    eye_c = (
        lax.broadcasted_iota(jnp.int32, (64, 64), 0) == lax.broadcasted_iota(jnp.int32, (64, 64), 1)
    ).astype(F32).astype(BF)
    cell_t = mm_nt(eye_c, per_cell).astype(BF)

    g_acc[...] = jnp.zeros_like(g_acc)

    def backward_step(s, carry):
        spread = mm(cell_t, members_of(s))
        slope = jnp.where(hidden[s] > 0, spread.astype(BF), jnp.zeros((), BF))
        moved = [slope]
        for b in range(1, 4):
            moved.append(
                jnp.concatenate(
                    [pltpu.roll(slope[:, r * LANES : (r + 1) * LANES], b, 1) for r in range(STEP)], axis=1
                )
            )
        g_acc[...] += mm_nt(wide_rows(s), jnp.concatenate(moved, axis=0))
        return carry

    lax.fori_loop(0, fr // STEP, backward_step, 0)

    g_acc[224:, :LANES] = g_head[:32]
    g_acc[224:, LANES:] = g_head[32:]
    gr = 256 // n_row
    owners = min(n_chip, gr // 16)
    every = owners == n_chip
    part[...] = g_acc[...].astype(BF).reshape(n_row, gr, 256)
    step_1 = [copy(part.at[o], got_1.at[row], s_1.at[o], r_1.at[row], dev) for o, dev in rows_of]
    for c in step_1:
        c.start()

    def when(chosen, run):
        if every:
            run()
        else:
            pl.when(chosen)(run)

    total = g_acc[pl.ds(row * gr, gr)]
    for o, dev in rows_of:
        copy(part.at[o], got_1.at[o], s_1.at[o], r_1.at[o], dev).wait_recv()
        total += got_1[pl.ds(o, 1)].reshape(gr, 256).astype(F32)
    part_2[...] = total.astype(BF).reshape(part_2.shape)
    step_2 = [copy(part_2.at[o], got_2.at[chip], s_2.at[o], r_2.at[chip], dev) for o, dev in chips]
    for (o, _), c in zip(chips, step_2):
        when(o < owners, c.start)
    across = [copy(got_4.at[row, chip], got_4.at[row, chip], s_3.at[o], r_3.at[chip], dev) for o, dev in chips]

    def own_chunk():
        got_2[pl.ds(chip, 1)] = part_2[pl.ds(chip, 1)]
        for o, dev in chips:
            copy(got_2.at[o], got_2.at[o], s_2.at[o], r_2.at[o], dev).wait_recv()
        total = got_2[0].astype(F32)
        for m in range(1, n_chip):
            total += got_2[m].astype(F32)
        got_4[row, pl.ds(chip, 1)] = total.astype(BF)[None]
        for c in across:
            c.start()

    when(chip < owners, own_chunk)

    def pass_on(o):
        return [copy(got_4.at[row, o], got_4.at[row, o], s_4.at[k, o], r_4.at[row, o], dev) for k, dev in rows_of]

    def start_all(copies):
        for c in copies:
            c.start()

    when(chip < owners, lambda: start_all(pass_on(chip)))
    for o, dev in reversed(chips):
        def arrived(o=o, dev=dev):
            copy(got_4.at[row, o], got_4.at[row, o], s_3.at[o], r_3.at[o], dev).wait_recv()
            start_all(pass_on(o))

        when(o < owners, arrived)
    for k, dev in rows_of:
        for o in range(owners):
            copy(got_4.at[k, o], got_4.at[k, o], s_4.at[k, o], r_4.at[k, o], dev).wait_recv()
    stem_out[...] = got_4[...].reshape(256, 256)

    for (o, _), c in zip(chips, step_2):
        when(o < owners, c.wait_send)
    when(chip < owners, lambda: [c.wait_send() for c in across] and None)
    for o in range(owners):
        for c in pass_on(o):
            c.wait_send()
    sends += step_1
    for c in sends:
        c.wait_send()

    @pl.when(col < n_col - 1)
    def _():
        to_right.wait_send()

    @pl.when(col > 0)
    def _():
        to_left.wait_send()

    @pl.when(row < n_row - 1)
    def _():
        down.wait_send()

    @pl.when(row > 0)
    def _():
        up.wait_send()


def finish(loss, stem, taps, loss_out, stem_out, head_out):
    loss_out[...] = loss[...]
    head_out[...] = unfold(stem[224:].astype(F32))
    bands = stem_out.shape[0]
    result = jnp.zeros((bands * 56, 64), F32)
    for b in range(4):
        result += mm(taps[b], stem[:, 64 * b : 64 * b + 64])
    stem_out[...] = result.reshape(bands, 7, 8, 64)[:, :, :7, :]


def solution(mesh):
    n_row, n_col, dates = mesh.shape["row"], mesh.shape["col"], mesh.shape["date"]

    def local(pixels, w_stem, w_head, pool_grid, neg_index, key_date):
        _, tiles, bands, height, width = pixels.shape
        fr, fc = height // 2, width // 2
        cells = fr // CELL * (fc // CELL)
        anchors = tiles * cells
        w_taps = jnp.transpose(w_stem, (1, 2, 3, 0))
        grid_t = pool_grid.T
        neg = jnp.transpose(neg_index[0], (1, 2, 0, 3)).reshape(anchors, -1)
        place = np.zeros((fc, LANES), np.float32)
        for j in range(fc):
            for t in range(tiles):
                place[j, t * HALF + j] = 1
        groups, half, n_chip = (bands + 1) // 2, 256 // n_row, n_col * dates
        owners = min(n_chip, half // 16)
        vmem = pl.BlockSpec(memory_space=pltpu.VMEM)
        dma = pltpu.SemaphoreType.DMA
        cols, edge, halo, rows, taps = tables(tiles, bands, height, width)
        operands = (
            pixels[0], edge, w_taps, taps, grid_t, jnp.asarray(place, BF), neg, cols, halo, rows,
            w_head, key_date,
        )
        operands = [pltpu.with_memory_space_constraint(x, pltpu.HBM) for x in operands]
        loss, stem, taps = pl.pallas_call(
            functools.partial(kernel, (tiles, bands, height, width, n_row, n_col, dates)),
            out_shape=(
                jax.ShapeDtypeStruct((fc // CELL, tiles, fr // CELL), F32),
                jax.ShapeDtypeStruct((256, 256), BF),
                jax.ShapeDtypeStruct(taps.shape, BF),
            ),
            in_specs=[pl.BlockSpec(memory_space=pltpu.HBM)] * len(operands),
            out_specs=(vmem, vmem, vmem),
            scratch_shapes=[pltpu.VMEM(x.shape, x.dtype) for x in operands[:3] + operands[4:-1]]
            + [pltpu.SMEM(key_date.shape, key_date.dtype)]
            + [
                pltpu.VMEM((bands, height, tiles * LANES), BF),
                pltpu.VMEM((2, groups, 16, height), BF),
                pltpu.VMEM((2, groups, 16, height), BF),
                pltpu.VMEM((height // 16, bands, 16, 2 * LANES), BF),
                pltpu.VMEM((height + 6, 2, 16, LANES), BF),
                pltpu.VMEM((256, 256), BF),
                pltpu.VMEM((fr, LANES), F32),
                pltpu.VMEM((neg.shape[1] * anchors // LANES, LANES), F32),
                pltpu.VMEM((anchors, anchors), F32),
                pltpu.VMEM((anchors, anchors), F32),
                pltpu.VMEM((dates, *neg.shape), BF),
                pltpu.VMEM((fr, anchors, LANES), BF),
                pltpu.VMEM((fr // STEP, 64, STEP * LANES), BF),
                pltpu.VMEM((anchors, 64), F32),
                pltpu.VMEM((dates, anchors // 2 + 8, LANES), BF),
                pltpu.VMEM((64, LANES), F32),
                pltpu.VMEM((256, 256), F32),
                pltpu.VMEM((n_row, half, 256), BF),
                pltpu.VMEM((n_row, half, 256), BF),
                pltpu.VMEM((owners, half // owners, 256), BF),
                pltpu.VMEM((n_chip, half // owners, 256), BF),
                pltpu.VMEM((n_row, owners, half // owners, 256), BF),
                dma((2,)), dma((2,)), dma((2,)), dma((2,)),
                dma((dates,)), dma((dates,)), dma((dates,)), dma((dates,)),
                dma((n_row,)), dma((n_row,)), dma((n_chip,)), dma((n_chip,)), dma((n_chip,)), dma((n_chip,)),
                dma((n_row, owners)), dma((n_row, owners)), dma((len(operands),)),
            ],
            compiler_params=pltpu.CompilerParams(
                collective_id=0, has_side_effects=True, vmem_limit_bytes=32 * 2**20
            ),
        )(*operands)
        loss, stem, head = pl.pallas_call(
            finish,
            out_shape=(
                jax.ShapeDtypeStruct(loss.shape, F32),
                jax.ShapeDtypeStruct((bands, 7, 7, 64), F32),
                jax.ShapeDtypeStruct((64, LANES), F32),
            ),
            in_specs=[vmem] * 3,
            out_specs=(vmem, vmem, vmem),
            compiler_params=pltpu.CompilerParams(vmem_limit_bytes=8 * 2**20),
        )(loss, stem, taps)
        loss = loss.transpose(1, 2, 0)[None]
        return loss, jnp.transpose(stem, (3, 0, 1, 2)), head

    return jax.shard_map(
        local,
        mesh=mesh,
        in_specs=(
            P(("groups", "date"), None, None, "row", "col"),
            P(),
            P(),
            P("row", "col"),
            P(("groups", "date"), None, "row", "col", None),
            P(),
        ),
        out_specs=(
            P(("groups", "date"), None, "row", "col"),
            P("groups", None, None, None),
            P("groups", None),
        ),
        check_vma=False,
    )
```

```python
import functools
import math

import jax
import jax.numpy as jnp
import numpy as np
from jax import lax
from jax.experimental import pallas as pl
from jax.experimental.pallas import tpu as pltpu
from jax.sharding import PartitionSpec as P

CELL = 8
TEMP = 0.2
EPS = 1e-06
STEP = 48
LANES = 128
HALF = 64

MESH = pl.DeviceIdType.MESH
BF = jnp.bfloat16
F32 = jnp.float32


def mm(left, right):
    return lax.dot_general(left, right, (((1,), (0,)), ((), ())), preferred_element_type=F32)


def split(array):
    high = array.astype(BF)
    return high, (array - high.astype(F32)).astype(BF)


def dot_3(left, right, over):
    (a, b), (c, d) = split(left), split(right)

    def one(x, y):
        return lax.dot_general(x, y, (over, ((), ())), preferred_element_type=F32)

    return one(a, c) + (one(a, d) + one(b, c))


def mm_high(left, right):
    return dot_3(left, right, ((1,), (0,)))


def fold(array):
    half = array.shape[0] // 2
    return jnp.concatenate([array[:half], array[half:]], axis=1)


def unfold(array):
    half = array.shape[1] // 2
    return jnp.concatenate([array[:, :half], array[:, half:]], axis=0)


def mm_nt(left, right):
    return lax.dot_general(left, right, (((1,), (1,)), ((), ())), preferred_element_type=F32)


def mm_tn(left, right):
    return lax.dot_general(left, right, (((0,), (0,)), ((), ())), preferred_element_type=F32)


def high_nt(left, right):
    return dot_3(left, right, ((1,), (1,)))


def high_tn(left, right):
    return dot_3(left, right, ((0,), (0,)))


def tables(tiles, bands, height, width):
    cols = np.zeros((tiles * LANES, 2 * LANES), np.float32)
    edge = np.zeros((2, 32, tiles * LANES), np.float32)
    halo = np.zeros((32, 2, 2 * LANES), np.float32)
    for t in range(tiles):
        for w in range(width):
            q = w + 3
            cols[t * LANES + w, (q % 2) * LANES + t * HALF + q // 2] = 1
        for k in range(3):
            for p in range(2):
                spot = p * 8 + t * 3 + k
                edge[p, spot, t * LANES + width - 3 + k] = 1
                edge[p, 16 + spot, t * LANES + k] = 1
                halo[spot, p, (k % 2) * LANES + t * HALF + k // 2] = 1
                q = width + 3 + k
                halo[16 + spot, p, (q % 2) * LANES + t * HALF + q // 2] = 1
    rows = np.zeros((16, 16, bands, 16), np.float32)
    for r in range(16):
        for c in range(bands):
            rows[r, c, c, r] = 1
    taps = np.zeros((4, bands, 7, 8, 8, 2, 16), np.float32)
    for b in range(4):
        for c in range(bands):
            for u in range(7):
                for pc in range(2):
                    if 2 * b + pc < 7:
                        taps[b, c, u, 2 * b + pc, u, pc, c] = 1
    tables = (
        cols, edge, halo.reshape(32, 4 * LANES), rows.reshape(256, bands * 16), taps.reshape(4, bands * 56, 256),
    )
    return [jnp.asarray(x, BF) for x in tables]


def kernel(
    sizes,
    *refs,
):
    n_in = 12
    sources, outs, taps = refs[:n_in], refs[n_in : n_in + 2], refs[n_in + 2]
    held, rest = refs[n_in + 3 : 2 * n_in + 2], refs[2 * n_in + 2 :]
    held = (*held[:3], taps, *held[3:])
    body(sizes, sources, held, *outs, *held, *rest)


def body(
    sizes, sources, held, loss_out, stem_out,
    pix, edge, w_taps, taps, grid_t, place, neg, cols, halo, rows, w_head, key_date,
    both_pix, pack, strips, blocks, image, w_all, gids, neg_t, count_t, count_s, negs, member, hidden,
    cell_count, keys, g_head, g_acc, part, got_1, part_2, got_2, got_4,
    s_col, r_col, s_row, r_row, s_key, r_key, s_neg, r_neg, s_1, r_1, s_2, r_2, s_3, r_3, s_4, r_4,
    s_in,
):
    tiles, bands, height, width, n_row, n_col, dates = sizes
    fr, fc = height // 2, width // 2
    cells = fr // CELL * (fc // CELL)
    anchors = tiles * cells
    n_mem = n_row * n_col
    row, col, date = lax.axis_index("row"), lax.axis_index("col"), lax.axis_index("date")

    fetches = [pltpu.make_async_copy(a, b, s_in.at[i]) for i, (a, b) in enumerate(zip(sources, held))]
    for c in fetches:
        c.start()
    barrier = pltpu.get_barrier_semaphore()

    def paired(value, mask, count):
        if count & (count - 1):
            return lax.rem(value + mask, count)
        k = 1
        while k < count:
            if mask & k:
                value = value + k - 2 * k * lax.rem(value // k, 2)
            k *= 2
        return value

    def others(name, count, mine):
        found = []
        for k in range(count - 1, 0, -1):
            other = paired(mine, k, count)
            found.append((other, {name: other}))
        return found

    rows_of, peers = others("row", n_row, row), others("date", dates, date)
    n_chip = n_col * dates
    chip = col * dates + date
    chips = []
    steps = [(a, b) for a in range(n_col) for b in range(dates) if a + b > 0]
    for a, b in sorted(steps, key=lambda step: (-sum(step), step)):
        to_col, to_date = paired(col, a, n_col), paired(date, b, dates)
        chips.append((to_col * dates + to_date, {"col": to_col, "date": to_date}))
    cols_of = others("col", n_col, col)
    for _, dev in rows_of + cols_of + peers:
        pl.semaphore_signal(barrier, inc=1, device_id=dev, device_id_type=MESH)

    fetches[0].wait()
    fetches[1].wait()

    for c in range(bands):
        flat = []
        for t in range(tiles):
            flat += [pix[t, c], jnp.zeros((height, LANES - width), BF)]
        both_pix[c] = jnp.concatenate(flat, axis=1)
    for g in range((bands + 1) // 2):
        ends = mm_nt(edge[0], both_pix[2 * g]).astype(BF)
        if 2 * g + 1 < bands:
            ends += mm_nt(edge[1], both_pix[2 * g + 1]).astype(BF)
        pack[0, g] = ends[:16]
        pack[1, g] = ends[16:]

    pl.semaphore_wait(barrier, len(rows_of) + len(cols_of) + len(peers))

    def copy(src, dst, send, recv, dev):
        return pltpu.make_async_remote_copy(
            src_ref=src, dst_ref=dst, send_sem=send, recv_sem=recv,
            device_id=dev, device_id_type=MESH,
        )

    to_right = copy(pack.at[0], strips.at[0], s_col.at[0], r_col.at[0], {"col": lax.rem(col + 1, n_col)})
    to_left = copy(pack.at[1], strips.at[1], s_col.at[1], r_col.at[1], {"col": lax.rem(col + n_col - 1, n_col)})
    down = copy(image.at[pl.ds(height, 3)], image.at[pl.ds(0, 3)], s_row.at[0], r_row.at[0], {"row": lax.rem(row + 1, n_row)})
    up = copy(image.at[pl.ds(3, 3)], image.at[pl.ds(height + 3, 3)], s_row.at[1], r_row.at[1], {"row": lax.rem(row + n_row - 1, n_row)})

    @pl.when(col < n_col - 1)
    def _():
        to_right.start()

    @pl.when(col > 0)
    def _():
        to_left.start()

    @pl.when(col == 0)
    def _():
        strips[0] = jnp.zeros(strips.shape[1:], BF)

    @pl.when(col == n_col - 1)
    def _():
        strips[1] = jnp.zeros(strips.shape[1:], BF)

    for c in fetches[2:]:
        c.wait()

    def own_band(c):
        wide = mm(both_pix[c], cols[...]).astype(BF)
        blocks[:, c] = wide.reshape(height // 16, 16, 2 * LANES)

    def own_bands(i, carry):
        for k in range(4):
            own_band(4 * i + k)
        return carry

    lax.fori_loop(0, bands // 4, own_bands, 0)
    for c in range(bands // 4 * 4, bands):
        own_band(c)

    w_flat = w_taps[...].astype(F32)
    w_flat = jnp.concatenate([w_flat, jnp.zeros((bands, 7, 1, 64), F32)], axis=2)
    w_flat = w_flat.reshape(bands * 56, 64).astype(BF)
    for b in range(4):
        w_all[64 * b : 64 * b + 64, :] = mm_tn(w_flat, taps[b]).astype(BF)
    lane = lax.broadcasted_iota(jnp.int32, (1, LANES), 1)
    inside = lax.rem(lane, HALF) < fc
    shift = jnp.where(inside, (lane // HALF) * cells, -1000).astype(F32)
    gids[...] = mm_tn(grid_t[...].astype(F32).astype(BF), place[...]) + shift
    sub = lax.broadcasted_iota(jnp.int32, (anchors, 1), 0)
    key_ids = (lax.rem(sub, tiles) * cells + sub // tiles).astype(F32)
    n_neg = neg.shape[1]
    rest = anchors - LANES
    split = LANES // rest
    per = n_neg // split

    def at(axis, shape):
        return lax.broadcasted_iota(jnp.int32, shape, axis)

    def ones_at(mask):
        return mask.astype(F32).astype(BF)

    square = (n_neg, n_neg)
    eye_n = ones_at(at(0, square) == at(1, square))
    fold_n = ones_at(at(0, (per, n_neg)) == lax.rem(at(1, (per, n_neg)), per))
    in_group = at(0, (LANES, n_neg)) // rest == at(1, (LANES, n_neg)) // per
    regroup = ones_at(lax.rem(at(0, (LANES, rest)), rest) == at(1, (LANES, rest)))

    def count_keys(index):
        neg_t[:n_neg] = mm_nt(eye_n, index[:LANES])
        tail = jnp.where(in_group, jnp.concatenate([index[LANES:].astype(F32)] * split, axis=0), 0.0)
        neg_t[n_neg:] = mm_nt(fold_n, tail.astype(BF))

        def count_step(s, total):
            for k in range(8):
                total += jnp.where(neg_t[pl.ds(s * 8 + k, 1), :] == key_ids, 1.0, 0.0)
            return total

        first = lax.fori_loop(0, n_neg // 8, count_step, jnp.zeros((anchors, LANES), F32))
        last = lax.fori_loop(n_neg // 8, (n_neg + per) // 8, count_step, jnp.zeros((anchors, LANES), F32))
        return jnp.concatenate([first, mm(last.astype(BF), regroup)], axis=1)

    def member_step(i, carry):
        for k in range(8):
            r = i * 8 + k
            here = jnp.where(gids[pl.ds(r, 1), :] == key_ids, 1.0, 0.0)
            member[r] = here.astype(BF)
            carry += here
        return carry

    found = lax.fori_loop(0, fr // 8, member_step, jnp.zeros((anchors, LANES), F32))
    cell_count[...] = jnp.broadcast_to(jnp.sum(found, axis=1, keepdims=True), (anchors, 64))

    def members_of(s):
        return jnp.concatenate([member[s * STEP + r] for r in range(STEP)], axis=1)

    @pl.when(col > 0)
    def _():
        copy(pack.at[0], strips.at[0], s_col.at[0], r_col.at[0], {"col": lax.rem(col + n_col - 1, n_col)}).wait_recv()

    @pl.when(col < n_col - 1)
    def _():
        copy(pack.at[1], strips.at[1], s_col.at[1], r_col.at[1], {"col": lax.rem(col + 1, n_col)}).wait_recv()

    negs[pl.ds(date, 1)] = neg[...].astype(F32).astype(BF)[None]
    sends = [copy(negs.at[date], negs.at[date], s_neg.at[o], r_neg.at[date], dev) for o, dev in peers]
    for c in sends:
        c.start()

    for g in range((bands + 1) // 2):
        ends = mm_tn(jnp.concatenate([strips[0, g], strips[1, g]], axis=0), halo[...]).astype(BF)
        for p in range(min(2, bands - 2 * g)):
            wide = ends[:, 2 * LANES * p : 2 * LANES * (p + 1)].reshape(height // 16, 16, 2 * LANES)
            blocks[:, 2 * g + p] += wide

    def image_step(k):
        out = mm(rows[...], blocks[k].reshape(bands * 16, 2 * LANES)).astype(BF)
        for pc in range(2):
            image[pl.ds(16 * k + 3, 16), pc] = out[:, pc * LANES : (pc + 1) * LANES].reshape(16, 16, LANES)

    image_step(height // 16 - 1)
    image_step(0)

    @pl.when(row < n_row - 1)
    def _():
        down.start()

    @pl.when(row > 0)
    def _():
        up.start()

    @pl.when(row == 0)
    def _():
        image[:3] = jnp.zeros((3, *image.shape[1:]), BF)

    @pl.when(row == n_row - 1)
    def _():
        image[height + 3 :] = jnp.zeros((3, *image.shape[1:]), BF)

    def image_pair(i, carry):
        image_step(2 * i + 1)
        image_step(2 * i + 2)
        return carry

    lax.fori_loop(0, height // 32 - 1, image_pair, 0)

    @pl.when(row > 0)
    def _():
        copy(image.at[pl.ds(height, 3)], image.at[pl.ds(0, 3)], s_row.at[0], r_row.at[0], {"row": lax.rem(row + n_row - 1, n_row)}).wait_recv()

    @pl.when(row < n_row - 1)
    def _():
        copy(image.at[pl.ds(3, 3)], image.at[pl.ds(height + 3, 3)], s_row.at[1], r_row.at[1], {"row": lax.rem(row + 1, n_row)}).wait_recv()

    def wide_rows(s):
        return jnp.concatenate(
            [image[pl.ds(2 * (s * STEP + r), 8)].reshape(256, LANES) for r in range(STEP)], axis=1
        )

    def forward_step(s, total):
        taps_out = mm(w_all[...], wide_rows(s))
        hid = []
        for r in range(STEP):
            part_r = taps_out[:, r * LANES : (r + 1) * LANES]
            stem = part_r[:64]
            for b in range(1, 4):
                stem += pltpu.roll(part_r[64 * b : 64 * b + 64], LANES - b, 1)
            hid.append(jnp.maximum(stem, 0.0).astype(BF))
        hid = jnp.concatenate(hid, axis=1)
        hidden[s] = hid
        return total + mm_nt(members_of(s), hid)

    sums = lax.fori_loop(0, fr // STEP, forward_step, jnp.zeros((anchors, 64), F32))
    counts = cell_count[...]
    pooled = sums / counts
    head = w_head[...]
    project = mm_high(pooled, head)
    length = jnp.sqrt(jnp.sum(project * project, axis=1, keepdims=True) + EPS)
    embed = project / length
    short = pooled / length
    folded = fold(short)
    mean = jnp.mean(folded, axis=0, keepdims=True)
    away = folded - mean
    base = [away]
    for _ in range(3):
        term = mean.astype(BF).astype(F32)
        base.append(term)
        mean = mean - term
    base.append(jnp.zeros((5, LANES), F32))
    keys[pl.ds(date, 1)] = jnp.concatenate(base, axis=0).astype(BF)[None]
    key_sends = [copy(keys.at[date], keys.at[date], s_key.at[o], r_key.at[date], dev) for o, dev in peers]
    for c in key_sends:
        c.start()
    back = high_nt(embed, head)
    for o, dev in peers:
        copy(negs.at[o], negs.at[o], s_neg.at[o], r_neg.at[o], dev).wait_recv()
    target = key_date[date]
    source = 0
    for d in range(dates):
        source = jnp.where(key_date[d] == date, d, source)
    count_t[...] = count_keys(negs[date])
    count_s[...] = count_keys(negs[source])
    for o, dev in peers:
        copy(keys.at[o], keys.at[o], s_key.at[o], r_key.at[o], dev).wait_recv()
    key_rows = anchors // 2

    def received(d):
        whole = keys[d].astype(F32)
        mean = whole[key_rows : key_rows + 1] + whole[key_rows + 1 : key_rows + 2] + whole[key_rows + 2 : key_rows + 3]
        return unfold(whole[:key_rows] + mean)

    key_short, own_short = received(target), received(source)
    same = lax.broadcasted_iota(jnp.int32, (anchors, anchors), 0) == lax.broadcasted_iota(
        jnp.int32, (anchors, anchors), 1
    )
    scale = 1.0 / math.sqrt(dates * anchors * n_mem)

    def contrast(scores, count):
        positive = jnp.sum(jnp.where(same, scores, 0.0), axis=0, keepdims=True)
        weights = count * jnp.exp(scores)
        exp_pos = jnp.exp(positive)
        denominator = exp_pos + jnp.sum(weights, axis=0, keepdims=True)
        d_scores = (scale / TEMP) * (
            weights / denominator + jnp.where(same, exp_pos / denominator - 1.0, 0.0)
        )
        return d_scores, jnp.log(denominator) - positive

    d_scores, losses = contrast(high_nt(key_short, back) / TEMP, count_t[...])
    d_source, _ = contrast(high_nt(back, own_short) / TEMP, count_s[...])
    grad_short = high_tn(d_scores, key_short) + mm_high(d_source, own_short)
    n_down, n_across = fr // CELL, fc // CELL
    wide = n_across * tiles
    spot = lax.broadcasted_iota(jnp.int32, (wide, anchors), 1)
    pick = jnp.where(lax.rem(spot, wide) == lax.broadcasted_iota(jnp.int32, (wide, anchors), 0), losses, 0.0)
    line = lax.broadcasted_iota(jnp.int32, (n_down, anchors), 1) // wide
    lines = (line == lax.broadcasted_iota(jnp.int32, (n_down, anchors), 0)).astype(F32)
    loss_out[...] = high_nt(pick, lines).reshape(n_across, tiles, n_down)
    grad_embed = mm_high(grad_short, head)
    grad_project = (
        grad_embed - embed * jnp.sum(embed * grad_embed, axis=1, keepdims=True)
    ) / length
    head_term = high_tn(pooled, grad_project)
    sends += key_sends
    g_head[...] = head_term
    per_cell = (high_nt(grad_project, head) / counts).astype(BF)
    eye_c = (
        lax.broadcasted_iota(jnp.int32, (64, 64), 0) == lax.broadcasted_iota(jnp.int32, (64, 64), 1)
    ).astype(F32).astype(BF)
    cell_t = mm_nt(eye_c, per_cell).astype(BF)

    g_acc[...] = jnp.zeros_like(g_acc)

    def backward_step(s, carry):
        spread = mm(cell_t, members_of(s))
        slope = jnp.where(hidden[s] > 0, spread.astype(BF), jnp.zeros((), BF))
        moved = [slope]
        for b in range(1, 4):
            moved.append(
                jnp.concatenate(
                    [pltpu.roll(slope[:, r * LANES : (r + 1) * LANES], b, 1) for r in range(STEP)], axis=1
                )
            )
        g_acc[...] += mm_nt(wide_rows(s), jnp.concatenate(moved, axis=0))
        return carry

    lax.fori_loop(0, fr // STEP, backward_step, 0)

    g_acc[224:, :LANES] = g_head[:32]
    g_acc[224:, LANES:] = g_head[32:]
    gr = 256 // n_row
    owners = min(n_chip, gr // 16)
    every = owners == n_chip
    part[...] = g_acc[...].astype(BF).reshape(n_row, gr, 256)
    step_1 = [copy(part.at[o], got_1.at[row], s_1.at[o], r_1.at[row], dev) for o, dev in rows_of]
    for c in step_1:
        c.start()

    def when(chosen, run):
        if every:
            run()
        else:
            pl.when(chosen)(run)

    total = g_acc[pl.ds(row * gr, gr)]
    for o, dev in rows_of:
        copy(part.at[o], got_1.at[o], s_1.at[o], r_1.at[o], dev).wait_recv()
        total += got_1[pl.ds(o, 1)].reshape(gr, 256).astype(F32)
    part_2[...] = total.astype(BF).reshape(part_2.shape)
    step_2 = [copy(part_2.at[o], got_2.at[chip], s_2.at[o], r_2.at[chip], dev) for o, dev in chips]
    for (o, _), c in zip(chips, step_2):
        when(o < owners, c.start)
    across = [copy(got_4.at[row, chip], got_4.at[row, chip], s_3.at[o], r_3.at[chip], dev) for o, dev in chips]

    def own_chunk():
        got_2[pl.ds(chip, 1)] = part_2[pl.ds(chip, 1)]
        for o, dev in chips:
            copy(got_2.at[o], got_2.at[o], s_2.at[o], r_2.at[o], dev).wait_recv()
        total = got_2[0].astype(F32)
        for m in range(1, n_chip):
            total += got_2[m].astype(F32)
        got_4[row, pl.ds(chip, 1)] = total.astype(BF)[None]
        for c in across:
            c.start()

    when(chip < owners, own_chunk)

    def pass_on(o):
        return [copy(got_4.at[row, o], got_4.at[row, o], s_4.at[k, o], r_4.at[row, o], dev) for k, dev in rows_of]

    def start_all(copies):
        for c in copies:
            c.start()

    when(chip < owners, lambda: start_all(pass_on(chip)))
    for o, dev in reversed(chips):
        def arrived(o=o, dev=dev):
            copy(got_4.at[row, o], got_4.at[row, o], s_3.at[o], r_3.at[o], dev).wait_recv()
            start_all(pass_on(o))

        when(o < owners, arrived)
    for k, dev in rows_of:
        for o in range(owners):
            copy(got_4.at[k, o], got_4.at[k, o], s_4.at[k, o], r_4.at[k, o], dev).wait_recv()
    stem_out[...] = got_4[...].reshape(256, 256)

    for (o, _), c in zip(chips, step_2):
        when(o < owners, c.wait_send)
    when(chip < owners, lambda: [c.wait_send() for c in across] and None)
    for o in range(owners):
        for c in pass_on(o):
            c.wait_send()
    sends += step_1
    for c in sends:
        c.wait_send()

    @pl.when(col < n_col - 1)
    def _():
        to_right.wait_send()

    @pl.when(col > 0)
    def _():
        to_left.wait_send()

    @pl.when(row < n_row - 1)
    def _():
        down.wait_send()

    @pl.when(row > 0)
    def _():
        up.wait_send()


def finish(loss, stem, taps, loss_out, stem_out, head_out):
    loss_out[...] = loss[...]
    head_out[...] = unfold(stem[224:].astype(F32))
    bands = stem_out.shape[0]
    result = jnp.zeros((bands * 56, 64), F32)
    for b in range(4):
        result += mm(taps[b], stem[:, 64 * b : 64 * b + 64])
    stem_out[...] = result.reshape(bands, 7, 8, 64)[:, :, :7, :]


def solution(mesh):
    n_row, n_col, dates = mesh.shape["row"], mesh.shape["col"], mesh.shape["date"]

    def local(pixels, w_stem, w_head, pool_grid, neg_index, key_date):
        _, tiles, bands, height, width = pixels.shape
        fr, fc = height // 2, width // 2
        cells = fr // CELL * (fc // CELL)
        anchors = tiles * cells
        w_taps = jnp.transpose(w_stem, (1, 2, 3, 0))
        grid_t = pool_grid.T
        neg = jnp.transpose(neg_index[0], (1, 2, 0, 3)).reshape(anchors, -1)
        place = np.zeros((fc, LANES), np.float32)
        for j in range(fc):
            for t in range(tiles):
                place[j, t * HALF + j] = 1
        groups, half, n_chip = (bands + 1) // 2, 256 // n_row, n_col * dates
        owners = min(n_chip, half // 16)
        vmem = pl.BlockSpec(memory_space=pltpu.VMEM)
        dma = pltpu.SemaphoreType.DMA
        cols, edge, halo, rows, taps = tables(tiles, bands, height, width)
        operands = (
            pixels[0], edge, w_taps, taps, grid_t, jnp.asarray(place, BF), neg, cols, halo, rows,
            w_head, key_date,
        )
        operands = [pltpu.with_memory_space_constraint(x, pltpu.HBM) for x in operands]
        loss, stem, taps = pl.pallas_call(
            functools.partial(kernel, (tiles, bands, height, width, n_row, n_col, dates)),
            out_shape=(
                jax.ShapeDtypeStruct((fc // CELL, tiles, fr // CELL), F32),
                jax.ShapeDtypeStruct((256, 256), BF),
                jax.ShapeDtypeStruct(taps.shape, BF),
            ),
            in_specs=[pl.BlockSpec(memory_space=pltpu.HBM)] * len(operands),
            out_specs=(vmem, vmem, vmem),
            scratch_shapes=[pltpu.VMEM(x.shape, x.dtype) for x in operands[:3] + operands[4:-1]]
            + [pltpu.SMEM(key_date.shape, key_date.dtype)]
            + [
                pltpu.VMEM((bands, height, tiles * LANES), BF),
                pltpu.VMEM((2, groups, 16, height), BF),
                pltpu.VMEM((2, groups, 16, height), BF),
                pltpu.VMEM((height // 16, bands, 16, 2 * LANES), BF),
                pltpu.VMEM((height + 6, 2, 16, LANES), BF),
                pltpu.VMEM((256, 256), BF),
                pltpu.VMEM((fr, LANES), F32),
                pltpu.VMEM((neg.shape[1] * anchors // LANES, LANES), F32),
                pltpu.VMEM((anchors, anchors), F32),
                pltpu.VMEM((anchors, anchors), F32),
                pltpu.VMEM((dates, *neg.shape), BF),
                pltpu.VMEM((fr, anchors, LANES), BF),
                pltpu.VMEM((fr // STEP, 64, STEP * LANES), BF),
                pltpu.VMEM((anchors, 64), F32),
                pltpu.VMEM((dates, anchors // 2 + 8, LANES), BF),
                pltpu.VMEM((64, LANES), F32),
                pltpu.VMEM((256, 256), F32),
                pltpu.VMEM((n_row, half, 256), BF),
                pltpu.VMEM((n_row, half, 256), BF),
                pltpu.VMEM((owners, half // owners, 256), BF),
                pltpu.VMEM((n_chip, half // owners, 256), BF),
                pltpu.VMEM((n_row, owners, half // owners, 256), BF),
                dma((2,)), dma((2,)), dma((2,)), dma((2,)),
                dma((dates,)), dma((dates,)), dma((dates,)), dma((dates,)),
                dma((n_row,)), dma((n_row,)), dma((n_chip,)), dma((n_chip,)), dma((n_chip,)), dma((n_chip,)),
                dma((n_row, owners)), dma((n_row, owners)), dma((len(operands),)),
            ],
            compiler_params=pltpu.CompilerParams(
                collective_id=0, has_side_effects=True, vmem_limit_bytes=32 * 2**20
            ),
        )(*operands)
        loss, stem, head = pl.pallas_call(
            finish,
            out_shape=(
                jax.ShapeDtypeStruct(loss.shape, F32),
                jax.ShapeDtypeStruct((bands, 7, 7, 64), F32),
                jax.ShapeDtypeStruct((64, LANES), F32),
            ),
            in_specs=[vmem] * 3,
            out_specs=(vmem, vmem, vmem),
            compiler_params=pltpu.CompilerParams(vmem_limit_bytes=8 * 2**20),
        )(loss, stem, taps)
        loss = loss.transpose(1, 2, 0)[None]
        return loss, jnp.transpose(stem, (3, 0, 1, 2)), head

    return jax.shard_map(
        local,
        mesh=mesh,
        in_specs=(
            P(("groups", "date"), None, None, "row", "col"),
            P(),
            P(),
            P("row", "col"),
            P(("groups", "date"), None, "row", "col", None),
            P(),
        ),
        out_specs=(
            P(("groups", "date"), None, "row", "col"),
            P("groups", None, None, None),
            P("groups", None),
        ),
        check_vma=False,
    )
```
